128 devices in a mesh: ctx: 16 (over y_hi, z, core), head: 8 (over y_lo, x).
Axes of the slice: x: 4, y: 4 (y_hi: 2, y_lo: 2; y = y_hi * 2 + y_lo), z: 4, core: 2. Of those that a mesh axis runs over, the one named last changes fastest.
Arguments:
- queries: bfloat16 [16384, 4096], P('ctx', 'head'), may hold values from -24 to 24
- key_states: bfloat16 [16384, 4096], P('ctx', 'head'), may hold values from -24 to 24
- value_states: bfloat16 [16384, 4096], P('ctx', 'head'), may hold values from -6 to 6
- out_grad: bfloat16 [16384, 4096], P('ctx', 'head'), may hold values from -6 to 6
- selected: int32 [256, 16], P('ctx'), may hold values from -1 to 255, as said below
Outputs:
- query_grad: bfloat16 [16384, 4096], P(('ctx', 'head'))
- key_grad: bfloat16 [16384, 4096], P(('ctx', 'head'))
- value_grad: bfloat16 [16384, 4096], P(('ctx', 'head'))
The draws below stay inside these ranges and needn't reach their ends.
Inputs may be any that keep to these rules, and one draw needn't show every extreme that they name: `selected`: row i holds 16 distinct entries, each a block index or -1; block i itself is always among them and every other block named comes before i. In the aligned groups of 16 rows, the blocks named that lie in another group's range number at most 1 for each other group, exactly 1 for every earlier group, and none for a later group.
All inputs are finite; a program needn't handle non-finite values.
Results may differ from the reference program's by a relative error of at most 0.011.
Values may be sent and summed in bfloat16 or wider, within the bound.
No kernel may reach another device: no remote copies, remote signals or barrier semaphores. Data moves between devices by JAX's collectives and lax.ppermute only.
A program may use at most 192 MiB of HBM per device.

```python
import jax
import jax.numpy as jnp
from jax import lax

HDIM = 128
HEAD_DEV = 4
BLOCK = 64
TOPK = 16
CAP = 1
HEADS = 32
TOKENS = 16384
BPD = 16
NBLK = 256
GROUP = 8


def draw_queries(key, part):
    shape = (TOKENS, HEADS * HDIM)
    base = jax.random.normal(jax.random.fold_in(key, 1), shape, jnp.float32)
    return jnp.clip(base, -24.0, 24.0).astype(jnp.bfloat16)


def draw_key_states(key, part):
    shape = (TOKENS, HEADS * HDIM)
    base = jax.random.normal(jax.random.fold_in(key, 2), shape, jnp.float32)
    return jnp.clip(base, -24.0, 24.0).astype(jnp.bfloat16)


def draw_selected(key, part):
    ranges = NBLK // BPD
    rows = jnp.arange(NBLK, dtype=jnp.int32)[:, None]
    cands = jnp.arange(NBLK, dtype=jnp.int32)[None, :]
    row_dev = rows // BPD
    cand_dev = cands // BPD
    cand_loc = cands % BPD
    within = rows % BPD
    pair_keys = jax.random.split(jax.random.fold_in(key, 3), ranges * ranges)
    orders = jax.vmap(lambda one: jax.random.permutation(one, BPD))(pair_keys).reshape(ranges, ranges, BPD)
    ranking = orders[row_dev, cand_dev, cand_loc]
    in_pool = (cand_dev < row_dev) & (ranking < CAP)
    pool_idx = cand_dev * CAP + ranking
    pool_size = jnp.maximum(row_dev * CAP, 1)
    mandated = in_pool & ((pool_idx == within % pool_size) | (pool_idx == (within + BPD) % pool_size))
    earlier_local = (cand_dev == row_dev) & (cands < rows)
    own_block = cands == rows
    priority = jnp.where(own_block, 3, jnp.where(mandated, 2, jnp.where(in_pool | earlier_local, 1, 0)))
    row_keys = jax.random.split(jax.random.fold_in(key, 5), NBLK)
    breaker = jax.vmap(lambda one: jax.random.permutation(one, NBLK))(row_keys).astype(jnp.int32)
    score = priority * NBLK + breaker
    values, indices = jax.lax.top_k(score, TOPK)
    return jnp.where(values >= NBLK, indices, -1).astype(jnp.int32)


def shard_levels(rng, dims, cuts, least, largest):
    def one(dim, shards_of):
        steps = jax.random.uniform(jax.random.fold_in(jax.random.fold_in(rng, 6), dim), (shards_of,), jnp.float32, least / len(cuts), largest / len(cuts))
        return jnp.repeat(jnp.exp(steps), dims[dim] // shards_of).reshape((-1,) + (1,) * (len(dims) - dim - 1))

    gain = one(*cuts[0])
    for cut in cuts[1:]:
        gain = gain * one(*cut)
    return gain


def scatter_about(own_key, extent, spread, bound, cuts=(), held_as=jnp.bfloat16):
    gain = shard_levels(own_key, extent, cuts, -0.22, 0.18) if cuts else 1.0
    drawn = jax.random.normal(own_key, extent, jnp.float32) * spread * gain
    return jnp.minimum(jnp.maximum(drawn, -bound), bound).astype(held_as)


def setup_inputs(seed: int = 0) -> dict:
    arg_keys = jax.random.split(jax.random.key(seed), 6)
    queries = draw_queries(jax.random.fold_in(arg_keys[5], 71), 0)
    key_states = draw_key_states(jax.random.fold_in(arg_keys[5], 71), 0)
    value_states = scatter_about(arg_keys[2], (TOKENS, HEADS * HDIM), 1.0, 6.0, ((0, 16), (1, 8)))
    out_grad = scatter_about(arg_keys[3], (TOKENS, HEADS * HDIM), 1.0, 6.0, ((0, 16), (1, 8)))
    selected = draw_selected(jax.random.fold_in(arg_keys[5], 71), 0)
    return {"queries": queries, "key_states": key_states, "value_states": value_states, "out_grad": out_grad, "selected": selected}


def block_grads(query_blk, key_blk, value_blk, grad_blk, select_blk, own_ids):
    count = query_blk.shape[0]
    scale = 1.0 / (HDIM ** 0.5)
    query_h = query_blk.astype(jnp.float32).reshape(count, BLOCK, HEAD_DEV, HDIM)
    key_h = key_blk.astype(jnp.float32).reshape(count, TOPK * BLOCK, HEAD_DEV, HDIM)
    value_h = value_blk.astype(jnp.float32).reshape(count, TOPK * BLOCK, HEAD_DEV, HDIM)
    grad_h = grad_blk.astype(jnp.float32).reshape(count, BLOCK, HEAD_DEV, HDIM)
    key_idx = jnp.arange(TOPK * BLOCK, dtype=jnp.int32)
    slot_of = key_idx // BLOCK
    key_pos = key_idx % BLOCK
    query_pos = jnp.arange(BLOCK, dtype=jnp.int32)
    block_of = select_blk[:, slot_of]
    allowed = (block_of >= 0)[:, None, :] & ((block_of != own_ids[:, None])[:, None, :] | (key_pos[None, None, :] <= query_pos[None, :, None]))
    scores = jnp.einsum('gqhd,gkhd->ghqk', query_h, key_h) * scale
    scores = jnp.where(allowed[:, None], scores, -1e30)
    highest = jnp.max(scores, axis=-1, keepdims=True)
    expo = jnp.exp(scores - highest)
    probs = expo / jnp.sum(expo, axis=-1, keepdims=True)
    probs_low = lax.optimization_barrier(probs.astype(jnp.bfloat16)).astype(jnp.float32)
    output = jnp.einsum('ghqk,gkhd->gqhd', probs_low, value_h)
    delta = jnp.einsum('gqhd,gqhd->ghq', grad_h, output)
    dprobs = jnp.einsum('gqhd,gkhd->ghqk', grad_h, value_h)
    dscores = probs * (dprobs - delta[..., None])
    dscores_low = lax.optimization_barrier(dscores.astype(jnp.bfloat16)).astype(jnp.float32)
    width = HEAD_DEV * HDIM
    dquery = (jnp.einsum('ghqk,gkhd->gqhd', dscores_low, key_h) * scale).astype(jnp.bfloat16)
    dkey = jnp.einsum('ghqk,gqhd->gkhd', dscores_low, query_h) * scale
    dvalue = jnp.einsum('ghqk,gqhd->gkhd', probs_low, grad_h)
    return dquery.reshape(count, BLOCK, width), dkey.reshape(count * TOPK, BLOCK, width), dvalue.reshape(count * TOPK, BLOCK, width)


def head_group(query_g, key_g, value_g, grad_g, selected):
    width = HEAD_DEV * HDIM
    query_b = query_g.reshape(NBLK, BLOCK, width)
    key_b = key_g.reshape(NBLK, BLOCK, width)
    value_b = value_g.reshape(NBLK, BLOCK, width)
    grad_b = grad_g.reshape(NBLK, BLOCK, width)

    def step(carry, span):
        bank_key, bank_value = carry
        start = (span * GROUP).astype(jnp.int32)
        query_c = lax.dynamic_slice_in_dim(query_b, start, GROUP, 0)
        grad_c = lax.dynamic_slice_in_dim(grad_b, start, GROUP, 0)
        select_c = lax.dynamic_slice_in_dim(selected, start, GROUP, 0)
        own_ids = start + jnp.arange(GROUP, dtype=jnp.int32)
        index = jnp.where(select_c >= 0, select_c, 0).astype(jnp.int32)
        key_c = key_b[index].reshape(GROUP, TOPK * BLOCK, width)
        value_c = value_b[index].reshape(GROUP, TOPK * BLOCK, width)
        dquery, dkey, dvalue = block_grads(query_c, key_c, value_c, grad_c, select_c, own_ids)
        flat = index.reshape(-1)
        bank_key = bank_key.at[flat].add(dkey)
        bank_value = bank_value.at[flat].add(dvalue)
        return (bank_key, bank_value), dquery

    zeros = jnp.zeros((NBLK, BLOCK, width), jnp.float32)
    (bank_key, bank_value), dquery = lax.scan(step, (zeros, zeros), jnp.arange(NBLK // GROUP, dtype=jnp.int32))
    return (dquery.reshape(TOKENS, width), bank_key.reshape(TOKENS, width).astype(jnp.bfloat16), bank_value.reshape(TOKENS, width).astype(jnp.bfloat16))


def reference(queries, key_states, value_states, out_grad, selected):
    groups = HEADS // HEAD_DEV
    width = HEAD_DEV * HDIM

    def split_heads(array):
        return array.reshape(TOKENS, groups, width).transpose(1, 0, 2)

    def one_group(packed):
        return head_group(packed[0], packed[1], packed[2], packed[3], selected)

    dquery, dkey, dvalue = lax.map(one_group, (split_heads(queries), split_heads(key_states), split_heads(value_states), split_heads(out_grad)))

    def join_heads(array):
        return array.transpose(1, 0, 2).reshape(TOKENS, HEADS * HDIM)

    return join_heads(dquery), join_heads(dkey), join_heads(dvalue)
```

```python
import jax
import jax.numpy as jnp
from jax import lax
from jax.experimental import pallas as pl
from jax.experimental.pallas import tpu as pltpu
from jax.sharding import PartitionSpec as P

HDIM = 128
BLOCK = 64
CHUNK = 256
SCALE = 1.0 / HDIM**0.5
LOG2E = 1.4426950408889634
EXP_SCALE = SCALE * LOG2E
MASKED = -1e30
F32 = jnp.float32
BF16 = jnp.bfloat16


def mm(a, b, dims):
    return lax.dot_general(a, b, (dims, ((), ())), preferred_element_type=F32)


NN = ((1,), (0,))
NT = ((1,), (1,))


def add_bias(scores, bias):
    keys, width = scores.shape
    blocks = keys // BLOCK
    return (scores.reshape(blocks, BLOCK, width) + bias[:, None, :]).reshape(keys, width)


def causal(scores):
    key_pos = lax.broadcasted_iota(jnp.int32, scores.shape, 0)
    query_pos = lax.broadcasted_iota(jnp.int32, scores.shape, 1)
    return jnp.where(key_pos <= query_pos, scores, MASKED)


def local_scores(k_ref, q, bias_ref, chunk):
    first = chunk * CHUNK
    last = first + CHUNK
    cols = pl.ds(first, CHUNK)
    diag = mm(k_ref[pl.ds(first, CHUNK), :], q, NT)
    diag = causal(add_bias(diag, bias_ref[pl.ds(first // BLOCK, CHUNK // BLOCK), cols]))
    if chunk == 0:
        return diag
    past = mm(k_ref[pl.ds(0, first), :], q, NT)
    past = add_bias(past, bias_ref[pl.ds(0, first // BLOCK), cols])
    return jnp.concatenate([past, diag], axis=0)


def local_stats_kernel(q_ref, do_ref, k_ref, v_ref, bias_ref, stat_ref):
    for chunk in range(q_ref.shape[0] // CHUNK):
        rows = pl.ds(chunk * CHUNK, CHUNK)
        end = (chunk + 1) * CHUNK
        s = local_scores(k_ref, q_ref[rows, :], bias_ref, chunk)
        dp = mm(v_ref[pl.ds(0, end), :], do_ref[rows, :], NT)
        top = jnp.max(s, axis=0, keepdims=True) * EXP_SCALE
        e = jnp.exp2(s * EXP_SCALE - top)
        stat_ref[0, 0:1, rows] = top
        stat_ref[0, 1:2, rows] = jnp.sum(e, axis=0, keepdims=True)
        stat_ref[0, 2:3, rows] = jnp.sum(e * dp, axis=0, keepdims=True)


def remote_kernel(q_ref, do_ref, k_ref, v_ref, bias_ref, stat_ref, dq_ref, grad_ref, full_ref, dk_acc, dv_acc):
    slots = k_ref.shape[0]
    keys = slots * BLOCK
    k = k_ref[...].reshape(keys, HDIM)
    v = v_ref[...].reshape(keys, HDIM)
    k_t = k.T
    for chunk in range(q_ref.shape[0] // CHUNK):
        rows = pl.ds(chunk * CHUNK, CHUNK)
        q = q_ref[rows, :]
        do = do_ref[rows, :]
        s = add_bias(mm(k, q, NT), bias_ref[:, rows])
        dp = mm(v, do, NT)
        top_loc = stat_ref[0, 0:1, rows]
        top = jnp.maximum(jnp.max(s, axis=0, keepdims=True) * EXP_SCALE, top_loc)
        e = jnp.exp2(s * EXP_SCALE - top)
        keep = jnp.exp2(top_loc - top)
        total = stat_ref[0, 1:2, rows] * keep + jnp.sum(e, axis=0, keepdims=True)
        dot = stat_ref[0, 2:3, rows] * keep + jnp.sum(e * dp, axis=0, keepdims=True)
        inv = 1.0 / total
        delta = dot * inv
        full_ref[0, 0:1, rows] = top
        full_ref[0, 1:2, rows] = inv
        full_ref[0, 2:3, rows] = delta
        p = e * inv
        ds = (p * (dp - delta)).astype(BF16)
        p = p.astype(BF16)
        dq_ref[0, :, rows] = mm(k_t, ds, NN)
        dk = mm(ds, q, NN)
        dv = mm(p, do, NN)
        if chunk == 0:
            dk_acc[...] = dk
            dv_acc[...] = dv
        else:
            dk_acc[...] += dk
            dv_acc[...] += dv
    grad_ref[:, 0:BLOCK, :] = (dk_acc[...] * SCALE).astype(BF16).reshape(slots, BLOCK, HDIM)
    grad_ref[:, BLOCK:, :] = dv_acc[...].astype(BF16).reshape(slots, BLOCK, HDIM)


def local_grads_kernel(q_ref, do_ref, k_ref, v_ref, bias_ref, full_ref, dqr_ref, dq_ref, dk_ref, dv_ref):
    k_t = k_ref[...].T
    for chunk in range(q_ref.shape[0] // CHUNK):
        rows = pl.ds(chunk * CHUNK, CHUNK)
        end = (chunk + 1) * CHUNK
        q = q_ref[rows, :]
        do = do_ref[rows, :]
        s = local_scores(k_ref, q, bias_ref, chunk)
        dp = mm(v_ref[pl.ds(0, end), :], do, NT)
        top = full_ref[0, 0:1, rows]
        inv = full_ref[0, 1:2, rows]
        delta = full_ref[0, 2:3, rows]
        p = jnp.exp2(s * EXP_SCALE - top) * inv
        ds = (p * (dp - delta)).astype(BF16)
        p = p.astype(BF16)
        dq = (dqr_ref[0, :, rows] + mm(k_t[:, :end], ds, NN)) * SCALE
        dq_ref[rows, :] = dq.T.astype(BF16)
        dk = mm(ds, q, NN)
        dv = mm(p, do, NN)
        if chunk == 0:
            dk_ref[rows, :] = dk
            dv_ref[rows, :] = dv
        else:
            past = pl.ds(0, chunk * CHUNK)
            dk_ref[past, :] += dk[: chunk * CHUNK]
            dv_ref[past, :] += dv[: chunk * CHUNK]
            dk_ref[rows, :] = dk[chunk * CHUNK :]
            dv_ref[rows, :] = dv[chunk * CHUNK :]


def gather_kernel(asks_ref, k_ref, v_ref, out_ref, sem):
    copies = []
    for slot in range(out_ref.shape[0]):
        rows = pl.ds(asks_ref[slot] * BLOCK, BLOCK)
        for part, src in enumerate((k_ref, v_ref)):
            copy = pltpu.make_async_copy(
                src.at[rows, :], out_ref.at[slot, pl.ds(part * BLOCK, BLOCK), :], sem.at[slot, part]
            )
            copy.start()
            copies.append(copy)
    for copy in copies:
        copy.wait()


def finish_kernel(asks_ref, dk_ref, dv_ref, back_ref, out_ref, acc):
    slots = back_ref.shape[0]
    acc[0] = dk_ref[...] * SCALE
    acc[1] = dv_ref[...]

    def add(slot, _):
        rows = pl.ds(pl.multiple_of(asks_ref[slot] * BLOCK, BLOCK), BLOCK)
        acc[0, rows, :] += back_ref[slot, 0:BLOCK, :].astype(F32)
        acc[1, rows, :] += back_ref[slot, BLOCK:, :].astype(F32)
        return 0

    lax.fori_loop(0, slots, add, 0)
    parts, _, per_part, width = out_ref.shape
    for part in range(parts):
        for which in range(2):
            out_ref[part, which] = acc[which, pl.ds(part * per_part, per_part), :].astype(BF16)


def params(**kwargs):
    return pltpu.CompilerParams(vmem_limit_bytes=48 << 20, **kwargs)


def per_device(queries, key_states, value_states, out_grad, selected):
    ranges = lax.axis_size("ctx")
    members = lax.axis_size("head")
    here = lax.axis_index("ctx")
    per_dev = selected.shape[0]
    tokens, width = queries.shape
    heads = width // HDIM
    ids = jnp.arange(ranges, dtype=jnp.int32)
    usable = selected >= 0
    owner = jnp.where(usable, selected // per_dev, -1)
    local_blk = jnp.where(usable, selected % per_dev, 0)
    from_range = owner[None] == ids[:, None, None]
    wanted = jnp.max(jnp.where(from_range, local_blk[None], 0), axis=(1, 2))
    asks = lax.all_to_all(wanted, "ctx", split_axis=0, concat_axis=0, tiled=True)

    blocks = jnp.arange(per_dev, dtype=jnp.int32)
    has_local = jnp.any(selected[None] == (here * per_dev + blocks)[:, None, None], axis=2)
    has_remote = jnp.any(from_range, axis=2) & (ids != here)[:, None]
    bias = jnp.where(jnp.concatenate([has_local, has_remote], axis=0), 0.0, MASKED).astype(F32)
    bias = jnp.repeat(bias, BLOCK, axis=1)
    bias_local, bias_remote = bias[:per_dev], bias[per_dev:]

    head_cols = pl.BlockSpec((tokens, HDIM), lambda h: (0, h))
    whole = lambda a: pl.BlockSpec(a.shape, lambda h: (0,) * len(a.shape))
    per_head = lambda shape: pl.BlockSpec((1,) + shape, lambda h: (h, 0, 0))
    pairs = tokens * tokens * heads
    in_any = pl.BlockSpec(memory_space=pl.ANY)

    sent = pl.pallas_call(
        gather_kernel,
        grid_spec=pltpu.PrefetchScalarGridSpec(
            num_scalar_prefetch=1,
            grid=(),
            in_specs=[in_any, in_any],
            out_specs=in_any,
            scratch_shapes=[pltpu.SemaphoreType.DMA((ranges, 2))],
        ),
        out_shape=jax.ShapeDtypeStruct((ranges, 2 * BLOCK, width), BF16),
    )(asks, key_states, value_states)
    got = lax.all_to_all(sent, "ctx", split_axis=0, concat_axis=0, tiled=True)

    stats = pl.pallas_call(
        local_stats_kernel,
        grid=(heads,),
        in_specs=[head_cols, head_cols, head_cols, head_cols, whole(bias_local)],
        out_specs=per_head((8, tokens)),
        out_shape=jax.ShapeDtypeStruct((heads, 8, tokens), F32),
        compiler_params=params(),
        cost_estimate=pl.CostEstimate(
            flops=2 * 2 * pairs * HDIM, bytes_accessed=4 * tokens * width * 2, transcendentals=pairs
        ),
    )(queries, out_grad, key_states, value_states, bias_local)

    slot_cols = lambda part: pl.BlockSpec((ranges, BLOCK, HDIM), lambda h: (0, part, h))
    remote_keys = ranges * BLOCK
    dq_remote, grads, full = pl.pallas_call(
        remote_kernel,
        grid=(heads,),
        in_specs=[
            head_cols,
            head_cols,
            slot_cols(0),
            slot_cols(1),
            whole(bias_remote),
            per_head((8, tokens)),
        ],
        out_specs=[
            per_head((HDIM, tokens)),
            pl.BlockSpec((ranges, 2 * BLOCK, HDIM), lambda h: (0, 0, h)),
            per_head((8, tokens)),
        ],
        out_shape=[
            jax.ShapeDtypeStruct((heads, HDIM, tokens), F32),
            jax.ShapeDtypeStruct((ranges, 2 * BLOCK, width), BF16),
            jax.ShapeDtypeStruct((heads, 8, tokens), F32),
        ],
        scratch_shapes=[pltpu.VMEM((remote_keys, HDIM), F32), pltpu.VMEM((remote_keys, HDIM), F32)],
        compiler_params=params(),
        cost_estimate=pl.CostEstimate(
            flops=5 * 2 * pairs * HDIM, bytes_accessed=8 * tokens * width * 2, transcendentals=pairs
        ),
    )(queries, out_grad, got, got, bias_remote, stats)
    back = lax.all_to_all(grads, "ctx", split_axis=0, concat_axis=0, tiled=True)

    dq, dk, dv = pl.pallas_call(
        local_grads_kernel,
        grid=(heads,),
        in_specs=[
            head_cols,
            head_cols,
            head_cols,
            head_cols,
            whole(bias_local),
            per_head((8, tokens)),
            per_head((HDIM, tokens)),
        ],
        out_specs=[head_cols, head_cols, head_cols],
        out_shape=[
            jax.ShapeDtypeStruct((tokens, width), BF16),
            jax.ShapeDtypeStruct((tokens, width), F32),
            jax.ShapeDtypeStruct((tokens, width), F32),
        ],
        compiler_params=params(),
        cost_estimate=pl.CostEstimate(
            flops=5 * 2 * pairs * HDIM, bytes_accessed=10 * tokens * width * 2, transcendentals=pairs
        ),
    )(queries, out_grad, key_states, value_states, bias_local, full, dq_remote)

    per_part = tokens // members
    dq_out = lax.all_to_all(
        dq.reshape(members, per_part, width), "head", split_axis=0, concat_axis=0, tiled=True
    )
    vmem = pl.BlockSpec(memory_space=pltpu.VMEM)
    totals = pl.pallas_call(
        finish_kernel,
        in_specs=[pl.BlockSpec(memory_space=pltpu.SMEM), vmem, vmem, vmem],
        out_specs=vmem,
        out_shape=jax.ShapeDtypeStruct((members, 2, per_part, width), BF16),
        scratch_shapes=[pltpu.VMEM((2, tokens, width), F32)],
        compiler_params=params(),
        cost_estimate=pl.CostEstimate(
            flops=4 * tokens * width, bytes_accessed=8 * tokens * width * 2, transcendentals=0
        ),
    )(asks, dk, dv, back)
    kv_out = lax.all_to_all(totals, "head", split_axis=0, concat_axis=0, tiled=True)
    query_out = dq_out.transpose(1, 0, 2).reshape(per_part, members * width)
    kv_out = kv_out.transpose(1, 2, 0, 3).reshape(2, per_part, members * width)
    return (query_out, kv_out[0], kv_out[1])


def solution(mesh):
    return jax.shard_map(
        per_device,
        mesh=mesh,
        in_specs=(
            P("ctx", "head"),
            P("ctx", "head"),
            P("ctx", "head"),
            P("ctx", "head"),
            P("ctx", None),
        ),
        out_specs=(P(("ctx", "head"), None), P(("ctx", "head"), None), P(("ctx", "head"), None)),
        check_vma=False,
    )
```

```python
import jax
import jax.numpy as jnp
from jax import lax
from jax.experimental import pallas as pl
from jax.experimental.pallas import tpu as pltpu
from jax.sharding import PartitionSpec as P

HDIM = 128
BLOCK = 64
CHUNK = 256
SCALE = 1.0 / HDIM**0.5
LOG2E = 1.4426950408889634
EXP_SCALE = SCALE * LOG2E
MASKED = -1e30
F32 = jnp.float32
BF16 = jnp.bfloat16


def mm(a, b, dims):
    return lax.dot_general(a, b, (dims, ((), ())), preferred_element_type=F32)


NN = ((1,), (0,))
NT = ((1,), (1,))


def add_bias(scores, bias):
    keys, width = scores.shape
    blocks = keys // BLOCK
    return (scores.reshape(blocks, BLOCK, width) + bias[:, None, :]).reshape(keys, width)


def causal(scores):
    key_pos = lax.broadcasted_iota(jnp.int32, scores.shape, 0)
    query_pos = lax.broadcasted_iota(jnp.int32, scores.shape, 1)
    return jnp.where(key_pos <= query_pos, scores, MASKED)


def local_scores(k_ref, q, bias_ref, chunk):
    first = chunk * CHUNK
    last = first + CHUNK
    cols = pl.ds(first, CHUNK)
    diag = mm(k_ref[pl.ds(first, CHUNK), :], q, NT)
    diag = causal(add_bias(diag, bias_ref[pl.ds(first // BLOCK, CHUNK // BLOCK), cols]))
    if chunk == 0:
        return diag
    past = mm(k_ref[pl.ds(0, first), :], q, NT)
    past = add_bias(past, bias_ref[pl.ds(0, first // BLOCK), cols])
    return jnp.concatenate([past, diag], axis=0)


def local_stats_kernel(q_ref, do_ref, k_ref, v_ref, bias_ref, stat_ref):
    for chunk in range(q_ref.shape[0] // CHUNK):
        rows = pl.ds(chunk * CHUNK, CHUNK)
        end = (chunk + 1) * CHUNK
        s = local_scores(k_ref, q_ref[rows, :], bias_ref, chunk)
        dp = mm(v_ref[pl.ds(0, end), :], do_ref[rows, :], NT)
        top = jnp.max(s, axis=0, keepdims=True) * EXP_SCALE
        e = jnp.exp2(s * EXP_SCALE - top)
        stat_ref[0, 0:1, rows] = top
        stat_ref[0, 1:2, rows] = jnp.sum(e, axis=0, keepdims=True)
        stat_ref[0, 2:3, rows] = jnp.sum(e * dp, axis=0, keepdims=True)


def remote_kernel(q_ref, do_ref, k_ref, v_ref, bias_ref, stat_ref, dq_ref, grad_ref, full_ref):
    slots = k_ref.shape[0] - 1
    keys = slots * BLOCK
    k = k_ref[0:slots].reshape(keys, HDIM)
    v = v_ref[0:slots].reshape(keys, HDIM)
    q = q_ref[...]
    do = do_ref[...]
    s = add_bias(mm(k, q, NT), bias_ref[0:slots, :])
    dp = mm(v, do, NT)
    top_loc = stat_ref[0, 0:1, :]
    top = jnp.maximum(jnp.max(s, axis=0, keepdims=True) * EXP_SCALE, top_loc)
    e = jnp.exp2(s * EXP_SCALE - top)
    keep = jnp.exp2(top_loc - top)
    total = stat_ref[0, 1:2, :] * keep + jnp.sum(e, axis=0, keepdims=True)
    dot = stat_ref[0, 2:3, :] * keep + jnp.sum(e * dp, axis=0, keepdims=True)
    inv = 1.0 / total
    delta = dot * inv
    full_ref[0, 0:1, :] = top
    full_ref[0, 1:2, :] = inv
    full_ref[0, 2:3, :] = delta
    p = e * inv
    ds = (p * (dp - delta)).astype(BF16)
    dq_ref[0] = mm(k.T, ds, NN)
    dk = mm(ds, q, NN) * SCALE
    dv = mm(p.astype(BF16), do, NN)
    grad_ref[0:slots, 0:BLOCK, :] = dk.astype(BF16).reshape(slots, BLOCK, HDIM)
    grad_ref[0:slots, BLOCK:, :] = dv.astype(BF16).reshape(slots, BLOCK, HDIM)
    grad_ref[slots] = jnp.zeros(grad_ref.shape[1:], BF16)


def local_grads_kernel(q_ref, do_ref, k_ref, v_ref, bias_ref, full_ref, dqr_ref, dq_ref, dk_ref, dv_ref):
    k_t = k_ref[...].T
    for chunk in range(q_ref.shape[0] // CHUNK):
        rows = pl.ds(chunk * CHUNK, CHUNK)
        end = (chunk + 1) * CHUNK
        q = q_ref[rows, :]
        do = do_ref[rows, :]
        s = local_scores(k_ref, q, bias_ref, chunk)
        dp = mm(v_ref[pl.ds(0, end), :], do, NT)
        top = full_ref[0, 0:1, rows]
        inv = full_ref[0, 1:2, rows]
        delta = full_ref[0, 2:3, rows]
        p = jnp.exp2(s * EXP_SCALE - top) * inv
        ds = (p * (dp - delta)).astype(BF16)
        p = p.astype(BF16)
        dq = (dqr_ref[0, :, rows] + mm(k_t[:, :end], ds, NN)) * SCALE
        parts = CHUNK // dq_ref.shape[2]
        dq_ref[pl.ds(chunk * parts, parts), 0] = dq.T.astype(BF16).reshape(parts, -1, HDIM)
        dk = mm(ds, q, NN)
        dv = mm(p, do, NN)
        if chunk == 0:
            dk_ref[rows, :] = dk
            dv_ref[rows, :] = dv
        else:
            past = pl.ds(0, chunk * CHUNK)
            dk_ref[past, :] += dk[: chunk * CHUNK]
            dv_ref[past, :] += dv[: chunk * CHUNK]
            dk_ref[rows, :] = dk[chunk * CHUNK :]
            dv_ref[rows, :] = dv[chunk * CHUNK :]


def gather_kernel(asks_ref, k_ref, v_ref, out_ref):
    for slot in range(out_ref.shape[0]):
        rows = pl.ds(pl.multiple_of(asks_ref[slot, 0] * BLOCK, BLOCK), BLOCK)
        out_ref[slot, 0:BLOCK, :] = k_ref[rows, :]
        out_ref[slot, BLOCK:, :] = v_ref[rows, :]


def finish_kernel(asks_ref, dk_ref, dv_ref, back_ref, _, out_ref, acc):
    acc[0] = dk_ref[...] * SCALE
    acc[1] = dv_ref[...]
    for slot in range(1, back_ref.shape[0]):
        rows = pl.ds(pl.multiple_of(asks_ref[slot, 0] * BLOCK, BLOCK), BLOCK)
        acc[0, rows, :] += back_ref[slot, 0:BLOCK, :].astype(F32)
        acc[1, rows, :] += back_ref[slot, BLOCK:, :].astype(F32)
    parts, _, per_part, _ = out_ref.shape
    for which in range(2):
        out_ref[:, which] = acc[which].astype(BF16).reshape(parts, per_part, HDIM)


def unpack_kernel(got_ref, *refs):
    outs, sem = refs[:-1], refs[-1]
    parts, _, _, width = got_ref.shape
    copies = []
    for part in range(parts):
        for which, out in enumerate(outs):
            cols = pl.ds(part * width, width)
            copy = pltpu.make_async_copy(got_ref.at[part, which], out.at[:, cols], sem.at[part, which])
            copy.start()
            copies.append(copy)
    for copy in copies:
        copy.wait()


def params(mib):
    return pltpu.CompilerParams(vmem_limit_bytes=mib << 20)


def per_device(queries, key_states, value_states, out_grad, selected):
    ranges = lax.axis_size("ctx")
    members = lax.axis_size("head")
    here = lax.axis_index("ctx")
    per_dev = selected.shape[0]
    tokens, width = queries.shape
    heads = width // HDIM
    ids = jnp.arange(ranges, dtype=jnp.int32)
    usable = selected >= 0
    owner = jnp.where(usable, selected // per_dev, -1)
    local_blk = jnp.where(usable, selected % per_dev, 0)
    from_range = owner[None] == ids[:, None, None]
    wanted = jnp.max(jnp.where(from_range, local_blk[None], 0), axis=(1, 2))
    wanted = jnp.broadcast_to(wanted[:, None], (ranges, HDIM))
    asks = lax.all_to_all(wanted, "ctx", split_axis=0, concat_axis=0, tiled=True)

    blocks = jnp.arange(per_dev, dtype=jnp.int32)
    has_local = jnp.any(selected[None] == (here * per_dev + blocks)[:, None, None], axis=2)
    has_remote = jnp.any(from_range, axis=2) & (ids != here)[:, None]
    bias = jnp.where(jnp.concatenate([has_local, has_remote], axis=0), 0.0, MASKED).astype(F32)
    bias = jnp.repeat(bias, BLOCK, axis=1)
    bias_local, bias_remote = bias[:per_dev], bias[per_dev:]

    head_cols = pl.BlockSpec((tokens, HDIM), lambda h: (0, h))
    whole = lambda a: pl.BlockSpec(a.shape, lambda h: (0,) * len(a.shape))
    per_head = lambda shape: pl.BlockSpec((1,) + shape, lambda h: (h, 0, 0))
    pairs = tokens * tokens * heads

    vmem = pl.BlockSpec(memory_space=pltpu.VMEM)
    smem = pl.BlockSpec(memory_space=pltpu.SMEM)
    sent = pl.pallas_call(
        gather_kernel,
        in_specs=[smem, vmem, vmem],
        out_specs=vmem,
        out_shape=jax.ShapeDtypeStruct((ranges, 2 * BLOCK, width), BF16),
        compiler_params=params(60),
    )(asks, key_states, value_states)
    got = lax.all_to_all(sent, "ctx", split_axis=0, concat_axis=0, tiled=True)

    stats = pl.pallas_call(
        local_stats_kernel,
        grid=(heads,),
        in_specs=[head_cols, head_cols, head_cols, head_cols, whole(bias_local)],
        out_specs=per_head((8, tokens)),
        out_shape=jax.ShapeDtypeStruct((heads, 8, tokens), F32),
        compiler_params=params(60),
        cost_estimate=pl.CostEstimate(
            flops=2 * 2 * pairs * HDIM, bytes_accessed=4 * tokens * width * 2, transcendentals=pairs
        ),
    )(queries, out_grad, key_states, value_states, bias_local)

    slot_cols = lambda part: pl.BlockSpec((ranges, BLOCK, HDIM), lambda h: (0, part, h))
    dq_remote, grads, full = pl.pallas_call(
        remote_kernel,
        grid=(heads,),
        in_specs=[
            head_cols,
            head_cols,
            slot_cols(0),
            slot_cols(1),
            whole(bias_remote),
            per_head((8, tokens)),
        ],
        out_specs=[
            per_head((HDIM, tokens)),
            pl.BlockSpec((ranges, 2 * BLOCK, HDIM), lambda h: (0, 0, h)),
            per_head((8, tokens)),
        ],
        out_shape=[
            jax.ShapeDtypeStruct((heads, HDIM, tokens), F32),
            jax.ShapeDtypeStruct((ranges, 2 * BLOCK, width), BF16),
            jax.ShapeDtypeStruct((heads, 8, tokens), F32),
        ],
        compiler_params=params(60),
        cost_estimate=pl.CostEstimate(
            flops=5 * 2 * pairs * HDIM, bytes_accessed=8 * tokens * width * 2, transcendentals=pairs
        ),
    )(queries, out_grad, got, got, bias_remote, stats)
    back = lax.all_to_all(grads, "ctx", split_axis=0, concat_axis=0, tiled=True)

    per_part = tokens // members
    mine, dk, dv = pl.pallas_call(
        local_grads_kernel,
        grid=(heads,),
        in_specs=[
            head_cols,
            head_cols,
            head_cols,
            head_cols,
            whole(bias_local),
            per_head((8, tokens)),
            per_head((HDIM, tokens)),
        ],
        out_specs=[
            pl.BlockSpec((members, 1, per_part, HDIM), lambda h: (0, 2, 0, h)),
            head_cols,
            head_cols,
        ],
        out_shape=[
            jax.ShapeDtypeStruct((members, 3, per_part, width), BF16),
            jax.ShapeDtypeStruct((tokens, width), F32),
            jax.ShapeDtypeStruct((tokens, width), F32),
        ],
        compiler_params=params(60),
        cost_estimate=pl.CostEstimate(
            flops=5 * 2 * pairs * HDIM, bytes_accessed=10 * tokens * width * 2, transcendentals=pairs
        ),
    )(queries, out_grad, key_states, value_states, bias_local, full, dq_remote)

    mine = pl.pallas_call(
        finish_kernel,
        grid=(heads,),
        in_specs=[
            smem,
            head_cols,
            head_cols,
            pl.BlockSpec((ranges, 2 * BLOCK, HDIM), lambda h: (0, 0, h)),
            pl.BlockSpec(memory_space=pl.ANY),
        ],
        out_specs=pl.BlockSpec((members, 2, per_part, HDIM), lambda h: (0, 0, 0, h)),
        out_shape=jax.ShapeDtypeStruct(mine.shape, BF16),
        scratch_shapes=[pltpu.VMEM((2, tokens, HDIM), F32)],
        input_output_aliases={4: 0},
        compiler_params=params(60),
        cost_estimate=pl.CostEstimate(
            flops=4 * tokens * width, bytes_accessed=8 * tokens * width * 2, transcendentals=0
        ),
    )(asks, dk, dv, back, mine)
    theirs = lax.all_to_all(mine, "head", split_axis=0, concat_axis=0, tiled=True)
    key_out, value_out, query_out = pl.pallas_call(
        unpack_kernel,
        in_specs=[vmem],
        out_specs=[pl.BlockSpec(memory_space=pl.ANY)] * 3,
        out_shape=[jax.ShapeDtypeStruct((per_part, members * width), BF16)] * 3,
        scratch_shapes=[pltpu.SemaphoreType.DMA((members, 3))],
        compiler_params=params(16),
    )(theirs)
    return (query_out, key_out, value_out)


def solution(mesh):
    return jax.shard_map(
        per_device,
        mesh=mesh,
        in_specs=(
            P("ctx", "head"),
            P("ctx", "head"),
            P("ctx", "head"),
            P("ctx", "head"),
            P("ctx", None),
        ),
        out_specs=(P(("ctx", "head"), None), P(("ctx", "head"), None), P(("ctx", "head"), None)),
        check_vma=False,
    )
```

```python
import jax
import jax.numpy as jnp
from jax import lax
from jax.experimental import pallas as pl
from jax.experimental.pallas import tpu as pltpu
from jax.sharding import PartitionSpec as P

HDIM = 128
BLOCK = 64
CHUNK = 256
SCALE = 1.0 / HDIM**0.5
LOG2E = 1.4426950408889634
EXP_SCALE = SCALE * LOG2E
MASKED = -1e30
HALVES = 2
LIMIT = 63
F32 = jnp.float32
BF16 = jnp.bfloat16


def mm(a, b, dims):
    return lax.dot_general(a, b, (dims, ((), ())), preferred_element_type=F32)


NN = ((1,), (0,))
NT = ((1,), (1,))


def add_bias(scores, bias):
    keys, width = scores.shape
    blocks = keys // BLOCK
    return (scores.reshape(blocks, BLOCK, width) + bias[:, None, :]).reshape(keys, width)


def causal(scores):
    key_pos = lax.broadcasted_iota(jnp.int32, scores.shape, 0)
    query_pos = lax.broadcasted_iota(jnp.int32, scores.shape, 1)
    return jnp.where(key_pos <= query_pos, scores, MASKED)


def local_scores(k_ref, q, bias_ref, chunk):
    first = chunk * CHUNK
    last = first + CHUNK
    cols = pl.ds(first, CHUNK)
    diag = mm(k_ref[pl.ds(first, CHUNK), :], q, NT)
    diag = causal(add_bias(diag, bias_ref[pl.ds(first // BLOCK, CHUNK // BLOCK), cols]))
    if chunk == 0:
        return diag
    past = mm(k_ref[pl.ds(0, first), :], q, NT)
    past = add_bias(past, bias_ref[pl.ds(0, first // BLOCK), cols])
    return jnp.concatenate([past, diag], axis=0)


def local_stats_kernel(q_ref, do_ref, k_ref, v_ref, bias_ref, stat_ref):
    for chunk in range(q_ref.shape[0] // CHUNK):
        rows = pl.ds(chunk * CHUNK, CHUNK)
        end = (chunk + 1) * CHUNK
        s = local_scores(k_ref, q_ref[rows, :], bias_ref, chunk)
        dp = mm(v_ref[pl.ds(0, end), :], do_ref[rows, :], NT)
        top = jnp.max(s, axis=0, keepdims=True) * EXP_SCALE
        e = jnp.exp2(s * EXP_SCALE - top)
        stat_ref[0, 0:1, rows] = top
        stat_ref[0, 1:2, rows] = jnp.sum(e, axis=0, keepdims=True)
        stat_ref[0, 2:3, rows] = jnp.sum(e * dp, axis=0, keepdims=True)


def remote_kernel(here_ref, q_ref, do_ref, k_ref, v_ref, bias_ref, stat_ref, *refs):
    *next_ref, dq_ref, grad_ref, full_ref = refs
    slots = k_ref.shape[0] - 1
    keys = slots * BLOCK
    k = k_ref[0:slots].reshape(keys, HDIM)
    v = v_ref[0:slots].reshape(keys, HDIM)
    q = q_ref[...]
    do = do_ref[...]
    s = add_bias(mm(k, q, NT), bias_ref[0:slots, :])
    dp = mm(v, do, NT)
    top_loc = stat_ref[0, 0:1, :]
    top = jnp.maximum(jnp.max(s, axis=0, keepdims=True) * EXP_SCALE, top_loc)
    e = jnp.exp2(s * EXP_SCALE - top)
    keep = jnp.exp2(top_loc - top)
    total = stat_ref[0, 1:2, :] * keep + jnp.sum(e, axis=0, keepdims=True)
    dot = stat_ref[0, 2:3, :] * keep + jnp.sum(e * dp, axis=0, keepdims=True)
    inv = 1.0 / total
    delta = dot * inv
    full_ref[0, 0:1, :] = top
    full_ref[0, 1:2, :] = inv
    full_ref[0, 2:3, :] = delta
    p = e * inv
    ds = (p * (dp - delta)).astype(BF16)
    dq_ref[0] = mm(k.T, ds, NN)
    dk = mm(ds, q, NN) * SCALE
    dv = mm(p.astype(BF16), do, NN)
    grad_ref[0:slots, 0:BLOCK, :] = dk.astype(BF16).reshape(slots, BLOCK, HDIM)
    grad_ref[0:slots, BLOCK:, :] = dv.astype(BF16).reshape(slots, BLOCK, HDIM)
    grad_ref[slots] = jnp.zeros(grad_ref.shape[1:], BF16)
    for ref in next_ref:
        for slot in range(slots + 1):

            @pl.when(slot > here_ref[0])
            def _():
                grad_ref[slot] = ref[slot]


def local_grads_kernel(q_ref, do_ref, k_ref, v_ref, bias_ref, full_ref, dqr_ref, dq_ref, dk_ref, dv_ref, dk_acc, dv_acc):
    k_t = k_ref[...].T
    for chunk in range(q_ref.shape[0] // CHUNK):
        rows = pl.ds(chunk * CHUNK, CHUNK)
        first = chunk * CHUNK
        end = first + CHUNK
        q = q_ref[rows, :]
        do = do_ref[rows, :]
        s = local_scores(k_ref, q, bias_ref, chunk)
        dp = mm(v_ref[pl.ds(0, end), :], do, NT)
        top = full_ref[0, 0:1, rows]
        inv = full_ref[0, 1:2, rows]
        delta = full_ref[0, 2:3, rows]
        p = jnp.exp2(s * EXP_SCALE - top) * inv
        ds = (p * (dp - delta)).astype(BF16)
        p = p.astype(BF16)
        dq = (dqr_ref[0, :, rows] + mm(k_t[:, :end], ds, NN)) * SCALE
        dq_ref[rows, :] = dq.T.astype(BF16)
        dk = mm(ds, q, NN)
        dv = mm(p, do, NN)
        if chunk > 0:
            dk_acc[0:first, :] += dk[:first]
            dv_acc[0:first, :] += dv[:first]
        dk_acc[rows, :] = dk[first:]
        dv_acc[rows, :] = dv[first:]
    dk_ref[...] = dk_acc[...] * SCALE
    dv_ref[...] = dv_acc[...]


def gather_kernel(asks_ref, k_ref, v_ref, *out_refs):
    for slot in range(out_refs[0].shape[0]):
        rows = pl.ds(pl.multiple_of(asks_ref[slot, 0] * BLOCK, BLOCK), BLOCK)
        for half, out_ref in enumerate(out_refs):
            width = out_ref.shape[2]
            cols = pl.ds(half * width, width)
            out_ref[slot, 0:BLOCK, :] = k_ref[rows, cols]
            out_ref[slot, BLOCK:, :] = v_ref[rows, cols]


def add_back(here_ref, asks_ref, dk_ref, dv_ref, back_ref, acc):
    acc[0] = dk_ref[...]
    acc[1] = dv_ref[...]
    for slot in range(1, back_ref.shape[0]):

        @pl.when(slot > here_ref[0])
        def _():
            rows = pl.ds(pl.multiple_of(asks_ref[slot, 0] * BLOCK, BLOCK), BLOCK)
            acc[0, rows, :] += back_ref[slot, 0:BLOCK, :].astype(F32)
            acc[1, rows, :] += back_ref[slot, BLOCK:, :].astype(F32)


def finish_kernel(here_ref, asks_ref, dq_ref, dk_ref, dv_ref, back_ref, out_ref, acc):
    add_back(here_ref, asks_ref, dk_ref, dv_ref, back_ref, acc)
    parts, _, per_part, _ = out_ref.shape
    for which in range(2):
        out_ref[:, which] = acc[which].astype(BF16).reshape(parts, per_part, HDIM)
    out_ref[:, 2] = dq_ref[...].reshape(parts, per_part, HDIM)


def finish_pieces_kernel(here_ref, asks_ref, me_ref, dq_ref, dk_ref, dv_ref, back_ref, *refs):
    *piece_refs, acc = refs
    add_back(here_ref, asks_ref, dk_ref, dv_ref, back_ref, acc)
    for d, piece_ref in enumerate(piece_refs):
        size = piece_ref.shape[1]
        rows = pl.ds(pl.multiple_of((me_ref[0] ^ d) * size, size), size)
        for which in range(2):
            piece_ref[which] = acc[which, rows, :].astype(BF16)
        piece_ref[2] = dq_ref[rows, :]


def unpack_kernel(half, got_ref, *refs):
    *outs, sem = refs
    outs = outs[-3:]
    parts, _, _, width = got_ref.shape
    copies = []
    for part in range(parts):
        for which, out in enumerate(outs):
            cols = pl.ds((part * HALVES + half) * width, width)
            copy = pltpu.make_async_copy(got_ref.at[part, which], out.at[:, cols], sem.at[part, which])
            copy.start()
            copies.append(copy)
    for copy in copies:
        copy.wait()


def unpack_pieces_kernel(half, me_ref, *refs):
    *refs, sem = refs
    pieces, outs = refs[:-3], refs[-3:]
    width = pieces[0].shape[2]
    copies = []
    for d, piece in enumerate(pieces):
        part = me_ref[0] ^ d
        for which, out in enumerate(outs):
            cols = pl.ds(pl.multiple_of((part * HALVES + half) * width, width), width)
            copy = pltpu.make_async_copy(piece.at[which], out.at[:, cols], sem.at[d, which])
            copy.start()
            copies.append(copy)
    for copy in copies:
        copy.wait()


def params(mib=LIMIT):
    return pltpu.CompilerParams(vmem_limit_bytes=mib << 20)


def swap(array, axis):
    return lax.all_to_all(array, axis, split_axis=0, concat_axis=0, tiled=True)


def per_device(queries, key_states, value_states, out_grad, selected):
    ranges = lax.axis_size("ctx")
    members = lax.axis_size("head")
    here = lax.axis_index("ctx")
    per_dev = selected.shape[0]
    tokens, width = queries.shape
    heads = width // HDIM
    half_heads = heads // HALVES
    half_width = width // HALVES
    per_part = tokens // members
    ids = jnp.arange(ranges, dtype=jnp.int32)
    usable = selected >= 0
    owner = jnp.where(usable, selected // per_dev, -1)
    local_blk = jnp.where(usable, selected % per_dev, 0)
    from_range = owner[None] == ids[:, None, None]
    wanted = jnp.max(jnp.where(from_range, local_blk[None], 0), axis=(1, 2))
    asks = swap(jnp.broadcast_to(wanted[:, None], (ranges, HDIM)), "ctx")
    here_arr = here.astype(jnp.int32).reshape(1)
    me_arr = lax.axis_index("head").astype(jnp.int32).reshape(1)

    vmem = pl.BlockSpec(memory_space=pltpu.VMEM)
    smem = pl.BlockSpec(memory_space=pltpu.SMEM)
    in_any = pl.BlockSpec(memory_space=pl.ANY)
    cols_at = lambda first: pl.BlockSpec((tokens, HDIM), lambda h: (0, first + h))
    whole = lambda a: pl.BlockSpec(a.shape, lambda h: (0,) * len(a.shape))
    per_head = lambda shape, first=0: pl.BlockSpec((1,) + shape, lambda h: (first + h, 0, 0))
    slot_cols = pl.BlockSpec((ranges, 2 * BLOCK, HDIM), lambda h: (0, 0, h))
    part_cols = lambda part: pl.BlockSpec((ranges, BLOCK, HDIM), lambda h: (0, part, h))
    pairs = tokens * tokens * half_heads
    cost = lambda dots, arrays: pl.CostEstimate(
        flops=dots * 2 * pairs * HDIM, bytes_accessed=arrays * tokens * half_width * 2, transcendentals=pairs
    )
    slots_half = jax.ShapeDtypeStruct((ranges, 2 * BLOCK, half_width), BF16)

    sent = pl.pallas_call(
        gather_kernel,
        in_specs=[smem, vmem, vmem],
        out_specs=[vmem] * HALVES,
        out_shape=[slots_half] * HALVES,
        compiler_params=params(),
    )(asks, key_states, value_states)
    selected, here, sent = lax.optimization_barrier((selected, here, sent))
    owner = jnp.where(selected >= 0, selected // per_dev, -1)
    from_range = owner[None] == ids[:, None, None]
    blocks = jnp.arange(per_dev, dtype=jnp.int32)
    has_local = jnp.any(selected[None] == (here * per_dev + blocks)[:, None, None], axis=2)
    has_remote = jnp.any(from_range, axis=2) & (ids != here)[:, None]
    bias = jnp.where(jnp.concatenate([has_local, has_remote], axis=0), 0.0, MASKED).astype(F32)
    bias = jnp.repeat(bias, BLOCK, axis=1)
    bias_local, bias_remote = bias[:per_dev], bias[per_dev:]
    got = swap(sent[0], "ctx")
    stats = pl.pallas_call(
        local_stats_kernel,
        grid=(heads,),
        in_specs=[cols_at(0)] * 4 + [whole(bias_local)],
        out_specs=per_head((8, tokens)),
        out_shape=jax.ShapeDtypeStruct((heads, 8, tokens), F32),
        compiler_params=params(),
        cost_estimate=cost(4, 8),
    )(queries, out_grad, key_states, value_states, bias_local)

    def remote(half, got, ahead):
        first = half * half_heads
        return pl.pallas_call(
            remote_kernel,
            grid=(half_heads,),
            in_specs=[
                smem,
                cols_at(first),
                cols_at(first),
                part_cols(0),
                part_cols(1),
                whole(bias_remote),
                per_head((8, tokens), first),
            ]
            + [slot_cols] * len(ahead),
            out_specs=[per_head((HDIM, tokens)), slot_cols, per_head((8, tokens))],
            out_shape=[
                jax.ShapeDtypeStruct((half_heads, HDIM, tokens), F32),
                slots_half,
                jax.ShapeDtypeStruct((half_heads, 8, tokens), F32),
            ],
            compiler_params=params(),
            cost_estimate=cost(5, 8),
        )(here_arr, queries, out_grad, got, got, bias_remote, stats, *ahead)

    def local(half, full, dq_remote):
        first = half * half_heads
        return pl.pallas_call(
            local_grads_kernel,
            grid=(half_heads,),
            in_specs=[cols_at(first)] * 4
            + [whole(bias_local), per_head((8, tokens)), per_head((HDIM, tokens))],
            out_specs=[cols_at(0)] * 3,
            out_shape=[
                jax.ShapeDtypeStruct((tokens, half_width), BF16),
                jax.ShapeDtypeStruct((tokens, half_width), F32),
                jax.ShapeDtypeStruct((tokens, half_width), F32),
            ],
            scratch_shapes=[pltpu.VMEM((tokens, HDIM), F32)] * 2,
            compiler_params=params(),
            cost_estimate=cost(5, 10),
        )(queries, out_grad, key_states, value_states, bias_local, full, dq_remote)

    finish_cost = pl.CostEstimate(
        flops=4 * tokens * half_width, bytes_accessed=16 * tokens * half_width, transcendentals=0
    )
    finish_acc = [pltpu.VMEM((2, tokens, HDIM), F32)]
    outs_shape = [jax.ShapeDtypeStruct((per_part, members * width), BF16)] * 3
    outs_sems = [pltpu.SemaphoreType.DMA((members, 3))]

    def finish(back, grads):
        return pl.pallas_call(
            finish_kernel,
            grid=(half_heads,),
            in_specs=[smem, smem] + [cols_at(0)] * 3 + [slot_cols],
            out_specs=pl.BlockSpec((members, 3, per_part, HDIM), lambda h: (0, 0, 0, h)),
            out_shape=jax.ShapeDtypeStruct((members, 3, per_part, half_width), BF16),
            scratch_shapes=finish_acc,
            compiler_params=params(),
            cost_estimate=finish_cost,
        )(here_arr, asks, *grads, back)

    def finish_pieces(back, grads):
        return pl.pallas_call(
            finish_pieces_kernel,
            grid=(half_heads,),
            in_specs=[smem, smem, smem] + [cols_at(0)] * 3 + [slot_cols],
            out_specs=[pl.BlockSpec((3, per_part, HDIM), lambda h: (0, 0, h))] * members,
            out_shape=[jax.ShapeDtypeStruct((3, per_part, half_width), BF16)] * members,
            scratch_shapes=finish_acc,
            compiler_params=params(),
            cost_estimate=finish_cost,
        )(here_arr, asks, me_arr, *grads, back)

    def unpack_pieces(half, pieces):
        return pl.pallas_call(
            lambda *refs: unpack_pieces_kernel(half, *refs),
            in_specs=[smem] + [vmem] * members,
            out_specs=[in_any] * 3,
            out_shape=outs_shape,
            scratch_shapes=outs_sems,
            compiler_params=params(16),
        )(me_arr, *pieces)

    def unpack(half, theirs, outs):
        return pl.pallas_call(
            lambda *refs: unpack_kernel(half, *refs),
            in_specs=[vmem] + [in_any] * len(outs),
            out_specs=[in_any] * 3,
            out_shape=outs_shape,
            scratch_shapes=outs_sems,
            input_output_aliases={1 + i: i for i in range(len(outs))},
            compiler_params=params(16),
        )(theirs, *outs)

    dq0, both, full0 = remote(0, got, sent[1:])
    both = swap(both, "ctx")
    own0 = local(0, full0, dq0)
    both, own0 = lax.optimization_barrier((both, own0))
    dq1, grads, full1 = remote(1, both, [])
    grads, both = lax.optimization_barrier((grads, both))
    back = swap(grads, "ctx")
    pieces = finish_pieces(both, own0)
    pieces = [pieces[0]] + [
        lax.ppermute(pieces[d], "head", [(i, i ^ d) for i in range(members)]) for d in range(1, members)
    ]
    own1 = local(1, full1, dq1)
    own1, pieces = lax.optimization_barrier((own1, pieces))
    outs = unpack_pieces(0, pieces)
    mine1 = finish(back, own1)
    key_out, value_out, query_out = unpack(1, swap(mine1, "head"), outs)
    return (query_out, key_out, value_out)


def solution(mesh):
    return jax.shard_map(
        per_device,
        mesh=mesh,
        in_specs=(
            P("ctx", "head"),
            P("ctx", "head"),
            P("ctx", "head"),
            P("ctx", "head"),
            P("ctx", None),
        ),
        out_specs=(P(("ctx", "head"), None), P(("ctx", "head"), None), P(("ctx", "head"), None)),
        check_vma=False,
    )
```

```python
import jax
import jax.numpy as jnp
from jax import lax
from jax.experimental import pallas as pl
from jax.experimental.pallas import tpu as pltpu
from jax.sharding import PartitionSpec as P

HDIM = 128
BLOCK = 64
CHUNK = 256
SCALE = 1.0 / HDIM**0.5
LOG2E = 1.4426950408889634
EXP_SCALE = SCALE * LOG2E
MASKED = -1e30
HALVES = 2
LIMIT = 63
KEY_TILE = 320
SAFE_EXPONENT = 64.0
F32 = jnp.float32
BF16 = jnp.bfloat16


def mm(a, b, dims):
    return lax.dot_general(a, b, (dims, ((), ())), preferred_element_type=F32)


NN = ((1,), (0,))
NT = ((1,), (1,))


def add_bias(scores, bias):
    keys, width = scores.shape
    blocks = keys // BLOCK
    return (scores.reshape(blocks, BLOCK, width) + bias[:, None, :]).reshape(keys, width)


def causal(scores):
    key_pos = lax.broadcasted_iota(jnp.int32, scores.shape, 0)
    query_pos = lax.broadcasted_iota(jnp.int32, scores.shape, 1)
    return jnp.where(key_pos <= query_pos, scores, MASKED)


def local_scores(k_ref, q, bias_ref, chunk):
    first = chunk * CHUNK
    last = first + CHUNK
    cols = pl.ds(first, CHUNK)
    diag = mm(k_ref[pl.ds(first, CHUNK), :], q, NT)
    diag = causal(add_bias(diag, bias_ref[pl.ds(first // BLOCK, CHUNK // BLOCK), cols]))
    if chunk == 0:
        return diag
    past = mm(k_ref[pl.ds(0, first), :], q, NT)
    past = add_bias(past, bias_ref[pl.ds(0, first // BLOCK), cols])
    return jnp.concatenate([past, diag], axis=0)


def local_stats_kernel(q_ref, do_ref, k_ref, v_ref, bias_ref, stat_ref):
    for chunk in range(q_ref.shape[0] // CHUNK):
        rows = pl.ds(chunk * CHUNK, CHUNK)
        end = (chunk + 1) * CHUNK
        s = local_scores(k_ref, q_ref[rows, :], bias_ref, chunk)
        dp = mm(v_ref[pl.ds(0, end), :], do_ref[rows, :], NT)
        top = jnp.max(s, axis=0, keepdims=True) * EXP_SCALE
        e = jnp.exp2(s * EXP_SCALE - top)
        stat_ref[0, 0:1, rows] = top
        stat_ref[0, 1:2, rows] = jnp.sum(e, axis=0, keepdims=True)
        stat_ref[0, 2:3, rows] = jnp.sum(e * dp, axis=0, keepdims=True)
        q = q_ref[rows, :].astype(F32)
        square = mm(jnp.ones((8, HDIM), BF16), (q * q).astype(BF16), NT)[0:1]
        stat_ref[0, 3:4, rows] = jnp.sqrt(square) * (1.02 * EXP_SCALE)


def remote_kernel(here_ref, q_ref, do_ref, k_ref, v_ref, bias_ref, stat_ref, *refs):
    *next_ref, dq_ref, grad_ref, full_ref, e_buf, dp_buf = refs
    slots = k_ref.shape[0] - 1
    keys = slots * BLOCK
    k = k_ref[0:slots].reshape(keys, HDIM)
    q = q_ref[...]
    do = do_ref[...]
    top_loc = stat_ref[0, 0:1, :]
    total_loc = stat_ref[0, 1:2, :]
    dot_loc = stat_ref[0, 2:3, :]

    def tiles():
        per_tile = KEY_TILE // BLOCK
        for tile in range(keys // KEY_TILE):
            at = pl.ds(tile * per_tile, per_tile)
            k_t = k_ref[at].reshape(KEY_TILE, HDIM)
            v_t = v_ref[at].reshape(KEY_TILE, HDIM)
            yield pl.ds(tile * KEY_TILE, KEY_TILE), at, mm(k_t, q, NT), mm(v_t, do, NT)

    def store(top, total, dot):
        inv = 1.0 / total
        full_ref[0, 0:1, :] = top
        full_ref[0, 1:2, :] = inv
        full_ref[0, 2:3, :] = dot * inv

    k32 = k.astype(F32)
    length = jnp.sum(k32 * k32, axis=1, keepdims=True)
    in_use = lax.broadcasted_iota(jnp.int32, length.shape, 0) < here_ref[0] * BLOCK
    longest = jnp.sqrt(jnp.max(jnp.where(in_use, length, 0.0), axis=0, keepdims=True))
    excess = jnp.max(stat_ref[0, 3:4, :] * longest - top_loc)

    @pl.when(excess < SAFE_EXPONENT)
    def _():
        total = total_loc
        dot = dot_loc
        for rows, at, s, dp in tiles():
            e = jnp.exp2(add_bias(s * EXP_SCALE, bias_ref[at, :] - top_loc))
            e_buf[rows, :] = e
            dp_buf[rows, :] = dp
            total += jnp.sum(e, axis=0, keepdims=True)
            dot += jnp.sum(e * dp, axis=0, keepdims=True)
        store(top_loc, total, dot)

    @pl.when(jnp.logical_not(excess < SAFE_EXPONENT))
    def _():
        top = top_loc
        for rows, at, s, dp in tiles():
            s = add_bias(s, bias_ref[at, :])
            e_buf[rows, :] = s
            dp_buf[rows, :] = dp
            top = jnp.maximum(top, jnp.max(s, axis=0, keepdims=True) * EXP_SCALE)
        e = jnp.exp2(e_buf[...] * EXP_SCALE - top)
        e_buf[...] = e
        keep = jnp.exp2(top_loc - top)
        total = total_loc * keep + jnp.sum(e, axis=0, keepdims=True)
        dot = dot_loc * keep + jnp.sum(e * dp_buf[...], axis=0, keepdims=True)
        store(top, total, dot)

    p = e_buf[...] * full_ref[0, 1:2, :]
    ds = (p * (dp_buf[...] - full_ref[0, 2:3, :])).astype(BF16)
    dq_ref[0] = mm(k.T, ds, NN)
    dk = mm(ds, q, NN) * SCALE
    dv = mm(p.astype(BF16), do, NN)
    grad_ref[0:slots, 0:BLOCK, :] = dk.astype(BF16).reshape(slots, BLOCK, HDIM)
    grad_ref[0:slots, BLOCK:, :] = dv.astype(BF16).reshape(slots, BLOCK, HDIM)
    grad_ref[slots] = jnp.zeros(grad_ref.shape[1:], BF16)
    for ref in next_ref:
        for slot in range(slots + 1):

            @pl.when(slot > here_ref[0])
            def _():
                grad_ref[slot] = ref[slot]


def local_grads_kernel(q_ref, do_ref, k_ref, v_ref, bias_ref, full_ref, dqr_ref, dq_ref, dk_ref, dv_ref, dk_acc, dv_acc):
    k_t = k_ref[...].T
    for chunk in range(q_ref.shape[0] // CHUNK):
        rows = pl.ds(chunk * CHUNK, CHUNK)
        first = chunk * CHUNK
        end = first + CHUNK
        q = q_ref[rows, :]
        do = do_ref[rows, :]
        s = local_scores(k_ref, q, bias_ref, chunk)
        dp = mm(v_ref[pl.ds(0, end), :], do, NT)
        top = full_ref[0, 0:1, rows]
        inv = full_ref[0, 1:2, rows]
        delta = full_ref[0, 2:3, rows]
        p = jnp.exp2(s * EXP_SCALE - top) * inv
        ds = (p * (dp - delta)).astype(BF16)
        p = p.astype(BF16)
        dq = (dqr_ref[0, :, rows] + mm(k_t[:, :end], ds, NN)) * SCALE
        dq_ref[rows, :] = dq.T.astype(BF16)
        dk = mm(ds, q, NN)
        dv = mm(p, do, NN)
        if chunk > 0:
            dk_acc[0:first, :] += dk[:first]
            dv_acc[0:first, :] += dv[:first]
        dk_acc[rows, :] = dk[first:]
        dv_acc[rows, :] = dv[first:]
    dk_ref[...] = dk_acc[...] * SCALE
    dv_ref[...] = dv_acc[...]


def gather_kernel(asks_ref, k_ref, v_ref, out_ref):
    for slot in range(out_ref.shape[0]):
        rows = pl.ds(pl.multiple_of(asks_ref[slot, 0] * BLOCK, BLOCK), BLOCK)
        out_ref[slot, 0:BLOCK, :] = k_ref[rows, :]
        out_ref[slot, BLOCK:, :] = v_ref[rows, :]


def add_back(here_ref, asks_ref, dk_ref, dv_ref, back_ref, acc):
    acc[0] = dk_ref[...]
    acc[1] = dv_ref[...]
    for slot in range(1, back_ref.shape[0]):

        @pl.when(slot > here_ref[0])
        def _():
            rows = pl.ds(pl.multiple_of(asks_ref[slot, 0] * BLOCK, BLOCK), BLOCK)
            acc[0, rows, :] += back_ref[slot, 0:BLOCK, :].astype(F32)
            acc[1, rows, :] += back_ref[slot, BLOCK:, :].astype(F32)


def finish_kernel(here_ref, asks_ref, dq_ref, dk_ref, dv_ref, back_ref, out_ref, acc):
    add_back(here_ref, asks_ref, dk_ref, dv_ref, back_ref, acc)
    parts, _, per_part, _ = out_ref.shape
    for which in range(2):
        out_ref[:, which] = acc[which].astype(BF16).reshape(parts, per_part, HDIM)
    out_ref[:, 2] = dq_ref[...].reshape(parts, per_part, HDIM)


def finish_pieces_kernel(here_ref, asks_ref, me_ref, dq_ref, dk_ref, dv_ref, back_ref, *refs):
    *piece_refs, acc = refs
    add_back(here_ref, asks_ref, dk_ref, dv_ref, back_ref, acc)
    for d, piece_ref in enumerate(piece_refs):
        size = piece_ref.shape[1]
        rows = pl.ds(pl.multiple_of((me_ref[0] ^ d) * size, size), size)
        for which in range(2):
            piece_ref[which] = acc[which, rows, :].astype(BF16)
        piece_ref[2] = dq_ref[rows, :]


def unpack_kernel(half, got_ref, *refs):
    *outs, sem = refs
    outs = outs[-3:]
    parts, _, _, width = got_ref.shape
    copies = []
    for part in range(parts):
        for which, out in enumerate(outs):
            cols = pl.ds((part * HALVES + half) * width, width)
            copy = pltpu.make_async_copy(got_ref.at[part, which], out.at[:, cols], sem.at[part, which])
            copy.start()
            copies.append(copy)
    for copy in copies:
        copy.wait()


def unpack_pieces_kernel(half, me_ref, *refs):
    *refs, sem = refs
    pieces, outs = refs[:-3], refs[-3:]
    width = pieces[0].shape[2]
    copies = []
    for d, piece in enumerate(pieces):
        part = me_ref[0] ^ d
        for which, out in enumerate(outs):
            cols = pl.ds(pl.multiple_of((part * HALVES + half) * width, width), width)
            copy = pltpu.make_async_copy(piece.at[which], out.at[:, cols], sem.at[d, which])
            copy.start()
            copies.append(copy)
    for copy in copies:
        copy.wait()


def params(mib=LIMIT):
    return pltpu.CompilerParams(vmem_limit_bytes=mib << 20)


def swap(array, axis):
    return lax.all_to_all(array, axis, split_axis=0, concat_axis=0, tiled=True)


def per_device(queries, key_states, value_states, out_grad, selected):
    ranges = lax.axis_size("ctx")
    members = lax.axis_size("head")
    here = lax.axis_index("ctx")
    per_dev = selected.shape[0]
    tokens, width = queries.shape
    heads = width // HDIM
    half_heads = heads // HALVES
    half_width = width // HALVES
    per_part = tokens // members
    ids = jnp.arange(ranges, dtype=jnp.int32)
    usable = selected >= 0
    owner = jnp.where(usable, selected // per_dev, -1)
    local_blk = jnp.where(usable, selected % per_dev, 0)
    from_range = owner[None] == ids[:, None, None]
    wanted = jnp.max(jnp.where(from_range, local_blk[None], 0), axis=(1, 2))
    me = lax.axis_index("head")
    wanted, here, me = lax.optimization_barrier((wanted, here, me))
    asks = swap(jnp.broadcast_to(wanted[:, None], (ranges, HDIM)), "ctx")
    here_arr = here.astype(jnp.int32).reshape(1)
    me_arr = me.astype(jnp.int32).reshape(1)

    vmem = pl.BlockSpec(memory_space=pltpu.VMEM)
    smem = pl.BlockSpec(memory_space=pltpu.SMEM)
    in_any = pl.BlockSpec(memory_space=pl.ANY)
    cols_at = lambda first: pl.BlockSpec((tokens, HDIM), lambda h: (0, first + h))
    whole = lambda a: pl.BlockSpec(a.shape, lambda h: (0,) * len(a.shape))
    per_head = lambda shape, first=0: pl.BlockSpec((1,) + shape, lambda h: (first + h, 0, 0))
    slot_cols = pl.BlockSpec((ranges, 2 * BLOCK, HDIM), lambda h: (0, 0, h))
    part_cols = lambda part: pl.BlockSpec((ranges, BLOCK, HDIM), lambda h: (0, part, h))
    pairs = tokens * tokens * half_heads
    cost = lambda dots, arrays: pl.CostEstimate(
        flops=dots * 2 * pairs * HDIM, bytes_accessed=arrays * tokens * half_width * 2, transcendentals=pairs
    )
    slots_half = jax.ShapeDtypeStruct((ranges, 2 * BLOCK, half_width), BF16)

    def gather(half, asks):
        return pl.pallas_call(
            gather_kernel,
            grid=(half_heads,),
            in_specs=[smem] + [cols_at(half * half_heads)] * 2,
            out_specs=slot_cols,
            out_shape=slots_half,
            compiler_params=params(),
        )(asks, key_states, value_states)

    sent = gather(0, asks)
    selected, here, asks, sent = lax.optimization_barrier((selected, here, asks, sent))
    owner = jnp.where(selected >= 0, selected // per_dev, -1)
    from_range = owner[None] == ids[:, None, None]
    blocks = jnp.arange(per_dev, dtype=jnp.int32)
    has_local = jnp.any(selected[None] == (here * per_dev + blocks)[:, None, None], axis=2)
    has_remote = jnp.any(from_range, axis=2) & (ids != here)[:, None]
    bias = jnp.where(jnp.concatenate([has_local, has_remote], axis=0), 0.0, MASKED).astype(F32)
    bias = jnp.repeat(bias, BLOCK, axis=1)
    bias_local, bias_remote = bias[:per_dev], bias[per_dev:]
    got = swap(sent, "ctx")
    ahead = gather(1, asks)
    stats = pl.pallas_call(
        local_stats_kernel,
        grid=(heads,),
        in_specs=[cols_at(0)] * 4 + [whole(bias_local)],
        out_specs=per_head((8, tokens)),
        out_shape=jax.ShapeDtypeStruct((heads, 8, tokens), F32),
        compiler_params=params(),
        cost_estimate=cost(4, 8),
    )(queries, out_grad, key_states, value_states, bias_local)

    def remote(half, got, ahead):
        first = half * half_heads
        return pl.pallas_call(
            remote_kernel,
            grid=(half_heads,),
            in_specs=[
                smem,
                cols_at(first),
                cols_at(first),
                part_cols(0),
                part_cols(1),
                whole(bias_remote),
                per_head((8, tokens), first),
            ]
            + [slot_cols] * len(ahead),
            out_specs=[per_head((HDIM, tokens)), slot_cols, per_head((8, tokens))],
            out_shape=[
                jax.ShapeDtypeStruct((half_heads, HDIM, tokens), F32),
                slots_half,
                jax.ShapeDtypeStruct((half_heads, 8, tokens), F32),
            ],
            scratch_shapes=[pltpu.VMEM(((ranges - 1) * BLOCK, tokens), F32)] * 2,
            compiler_params=params(),
            cost_estimate=cost(5, 8),
        )(here_arr, queries, out_grad, got, got, bias_remote, stats, *ahead)

    def local(half, full, dq_remote):
        first = half * half_heads
        return pl.pallas_call(
            local_grads_kernel,
            grid=(half_heads,),
            in_specs=[cols_at(first)] * 4
            + [whole(bias_local), per_head((8, tokens)), per_head((HDIM, tokens))],
            out_specs=[cols_at(0)] * 3,
            out_shape=[
                jax.ShapeDtypeStruct((tokens, half_width), BF16),
                jax.ShapeDtypeStruct((tokens, half_width), F32),
                jax.ShapeDtypeStruct((tokens, half_width), F32),
            ],
            scratch_shapes=[pltpu.VMEM((tokens, HDIM), F32)] * 2,
            compiler_params=params(),
            cost_estimate=cost(5, 10),
        )(queries, out_grad, key_states, value_states, bias_local, full, dq_remote)

    finish_cost = pl.CostEstimate(
        flops=4 * tokens * half_width, bytes_accessed=16 * tokens * half_width, transcendentals=0
    )
    finish_acc = [pltpu.VMEM((2, tokens, HDIM), F32)]
    outs_shape = [jax.ShapeDtypeStruct((per_part, members * width), BF16)] * 3
    outs_sems = [pltpu.SemaphoreType.DMA((members, 3))]

    def finish(back, grads):
        return pl.pallas_call(
            finish_kernel,
            grid=(half_heads,),
            in_specs=[smem, smem] + [cols_at(0)] * 3 + [slot_cols],
            out_specs=pl.BlockSpec((members, 3, per_part, HDIM), lambda h: (0, 0, 0, h)),
            out_shape=jax.ShapeDtypeStruct((members, 3, per_part, half_width), BF16),
            scratch_shapes=finish_acc,
            compiler_params=params(),
            cost_estimate=finish_cost,
        )(here_arr, asks, *grads, back)

    def finish_pieces(back, grads):
        return pl.pallas_call(
            finish_pieces_kernel,
            grid=(half_heads,),
            in_specs=[smem, smem, smem] + [cols_at(0)] * 3 + [slot_cols],
            out_specs=[pl.BlockSpec((3, per_part, HDIM), lambda h: (0, 0, h))] * members,
            out_shape=[jax.ShapeDtypeStruct((3, per_part, half_width), BF16)] * members,
            scratch_shapes=finish_acc,
            compiler_params=params(),
            cost_estimate=finish_cost,
        )(here_arr, asks, me_arr, *grads, back)

    def unpack_pieces(half, pieces):
        return pl.pallas_call(
            lambda *refs: unpack_pieces_kernel(half, *refs),
            in_specs=[smem] + [vmem] * members,
            out_specs=[in_any] * 3,
            out_shape=outs_shape,
            scratch_shapes=outs_sems,
            compiler_params=params(16),
        )(me_arr, *pieces)

    def unpack(half, theirs, outs):
        return pl.pallas_call(
            lambda *refs: unpack_kernel(half, *refs),
            in_specs=[vmem] + [in_any] * len(outs),
            out_specs=[in_any] * 3,
            out_shape=outs_shape,
            scratch_shapes=outs_sems,
            input_output_aliases={1 + i: i for i in range(len(outs))},
            compiler_params=params(16),
        )(theirs, *outs)

    dq0, both, full0 = remote(0, got, [ahead])
    both = swap(both, "ctx")
    own0 = local(0, full0, dq0)
    both, own0 = lax.optimization_barrier((both, own0))
    dq1, grads, full1 = remote(1, both, [])
    grads, both = lax.optimization_barrier((grads, both))
    back = swap(grads, "ctx")
    pieces = finish_pieces(both, own0)
    pieces = [pieces[0]] + [
        lax.ppermute(pieces[d], "head", [(i, i ^ d) for i in range(members)]) for d in range(1, members)
    ]
    own1 = local(1, full1, dq1)
    own1, pieces = lax.optimization_barrier((own1, pieces))
    outs = unpack_pieces(0, pieces)
    mine1 = finish(back, own1)
    key_out, value_out, query_out = unpack(1, swap(mine1, "head"), outs)
    return (query_out, key_out, value_out)


def solution(mesh):
    return jax.shard_map(
        per_device,
        mesh=mesh,
        in_specs=(
            P("ctx", "head"),
            P("ctx", "head"),
            P("ctx", "head"),
            P("ctx", "head"),
            P("ctx", None),
        ),
        out_specs=(P(("ctx", "head"), None), P(("ctx", "head"), None), P(("ctx", "head"), None)),
        check_vma=False,
    )
```

```python
import jax
import jax.numpy as jnp
from jax import lax
from jax.experimental import pallas as pl
from jax.experimental.pallas import tpu as pltpu
from jax.sharding import PartitionSpec as P

HDIM = 128
BLOCK = 64
CHUNK = 256
SCALE = 1.0 / HDIM**0.5
LOG2E = 1.4426950408889634
EXP_SCALE = SCALE * LOG2E
MASKED = -1e30
HALVES = 2
LIMIT = 63
KEY_TILE = 960
SAFE_EXPONENT = 64.0
F32 = jnp.float32
BF16 = jnp.bfloat16


def mm(a, b, dims):
    return lax.dot_general(a, b, (dims, ((), ())), preferred_element_type=F32)


NN = ((1,), (0,))
NT = ((1,), (1,))


def add_bias(scores, bias):
    keys, width = scores.shape
    blocks = keys // BLOCK
    return (scores.reshape(blocks, BLOCK, width) + bias[:, None, :]).reshape(keys, width)


def causal(scores):
    key_pos = lax.broadcasted_iota(jnp.int32, scores.shape, 0)
    query_pos = lax.broadcasted_iota(jnp.int32, scores.shape, 1)
    return jnp.where(key_pos <= query_pos, scores, MASKED)


def local_scores(k_ref, q, bias_ref, chunk):
    first = chunk * CHUNK
    last = first + CHUNK
    cols = pl.ds(first, CHUNK)
    diag = mm(k_ref[pl.ds(first, CHUNK), :], q, NT)
    diag = causal(add_bias(diag, bias_ref[pl.ds(first // BLOCK, CHUNK // BLOCK), cols]))
    if chunk == 0:
        return diag
    past = mm(k_ref[pl.ds(0, first), :], q, NT)
    past = add_bias(past, bias_ref[pl.ds(0, first // BLOCK), cols])
    return jnp.concatenate([past, diag], axis=0)


def local_stats_kernel(q_ref, do_ref, k_ref, v_ref, bias_ref, stat_ref):
    for chunk in range(q_ref.shape[0] // CHUNK):
        rows = pl.ds(chunk * CHUNK, CHUNK)
        end = (chunk + 1) * CHUNK
        s = local_scores(k_ref, q_ref[rows, :], bias_ref, chunk)
        dp = mm(v_ref[pl.ds(0, end), :], do_ref[rows, :], NT)
        top = jnp.max(s, axis=0, keepdims=True) * EXP_SCALE
        e = jnp.exp2(s * EXP_SCALE - top)
        stat_ref[0, 0:1, rows] = top
        stat_ref[0, 1:2, rows] = jnp.sum(e, axis=0, keepdims=True)
        stat_ref[0, 2:3, rows] = jnp.sum(e * dp, axis=0, keepdims=True)
        q = q_ref[rows, :].astype(F32)
        square = mm(jnp.ones((8, HDIM), BF16), (q * q).astype(BF16), NT)[0:1]
        stat_ref[0, 3:4, rows] = jnp.sqrt(square) * (1.02 * EXP_SCALE)


def remote_kernel(here_ref, q_ref, do_ref, k_ref, v_ref, bias_ref, stat_ref, *refs):
    *next_ref, dq_ref, grad_ref, full_ref, e_buf, dp_buf = refs
    slots = k_ref.shape[0] - 1
    keys = slots * BLOCK
    k = k_ref[0:slots].reshape(keys, HDIM)
    q = q_ref[...]
    do = do_ref[...]
    top_loc = stat_ref[0, 0:1, :]
    total_loc = stat_ref[0, 1:2, :]
    dot_loc = stat_ref[0, 2:3, :]

    def tiles():
        per_tile = KEY_TILE // BLOCK
        for tile in range(keys // KEY_TILE):
            at = pl.ds(tile * per_tile, per_tile)
            k_t = k_ref[at].reshape(KEY_TILE, HDIM)
            v_t = v_ref[at].reshape(KEY_TILE, HDIM)
            yield pl.ds(tile * KEY_TILE, KEY_TILE), at, mm(k_t, q, NT), mm(v_t, do, NT)

    def store(top, total, dot):
        inv = 1.0 / total
        full_ref[0, 0:1, :] = top
        full_ref[0, 1:2, :] = inv
        full_ref[0, 2:3, :] = dot * inv

    k32 = k.astype(F32)
    length = jnp.sum(k32 * k32, axis=1, keepdims=True)
    in_use = lax.broadcasted_iota(jnp.int32, length.shape, 0) < here_ref[0] * BLOCK
    longest = jnp.sqrt(jnp.max(jnp.where(in_use, length, 0.0), axis=0, keepdims=True))
    excess = jnp.max(stat_ref[0, 3:4, :] * longest - top_loc)

    @pl.when(excess < SAFE_EXPONENT)
    def _():
        total = total_loc
        dot = dot_loc
        for rows, at, s, dp in tiles():
            e = jnp.exp2(add_bias(s * EXP_SCALE, bias_ref[at, :] - top_loc))
            e_buf[rows, :] = e
            dp_buf[rows, :] = dp
            total += jnp.sum(e, axis=0, keepdims=True)
            dot += jnp.sum(e * dp, axis=0, keepdims=True)
        store(top_loc, total, dot)

    @pl.when(jnp.logical_not(excess < SAFE_EXPONENT))
    def _():
        top = top_loc
        for rows, at, s, dp in tiles():
            s = add_bias(s, bias_ref[at, :])
            e_buf[rows, :] = s
            dp_buf[rows, :] = dp
            top = jnp.maximum(top, jnp.max(s, axis=0, keepdims=True) * EXP_SCALE)
        e = jnp.exp2(e_buf[...] * EXP_SCALE - top)
        e_buf[...] = e
        keep = jnp.exp2(top_loc - top)
        total = total_loc * keep + jnp.sum(e, axis=0, keepdims=True)
        dot = dot_loc * keep + jnp.sum(e * dp_buf[...], axis=0, keepdims=True)
        store(top, total, dot)

    p = e_buf[...] * full_ref[0, 1:2, :]
    ds = (p * (dp_buf[...] - full_ref[0, 2:3, :])).astype(BF16)
    dq_ref[0] = mm(k.T, ds, NN)
    dk = mm(ds, q, NN) * SCALE
    dv = mm(p.astype(BF16), do, NN)
    grad_ref[0:slots, 0:BLOCK, :] = dk.astype(BF16).reshape(slots, BLOCK, HDIM)
    grad_ref[0:slots, BLOCK:, :] = dv.astype(BF16).reshape(slots, BLOCK, HDIM)
    grad_ref[slots] = jnp.zeros(grad_ref.shape[1:], BF16)
    for ref in next_ref:
        for slot in range(slots + 1):

            @pl.when(slot > here_ref[0])
            def _():
                grad_ref[slot] = ref[slot]


def local_grads_kernel(q_ref, do_ref, k_ref, v_ref, bias_ref, full_ref, dqr_ref, dq_ref, dk_ref, dv_ref, dk_acc, dv_acc):
    k_t = k_ref[...].T
    for chunk in range(q_ref.shape[0] // CHUNK):
        rows = pl.ds(chunk * CHUNK, CHUNK)
        first = chunk * CHUNK
        end = first + CHUNK
        q = q_ref[rows, :]
        do = do_ref[rows, :]
        s = local_scores(k_ref, q, bias_ref, chunk)
        dp = mm(v_ref[pl.ds(0, end), :], do, NT)
        top = full_ref[0, 0:1, rows]
        inv = full_ref[0, 1:2, rows]
        delta = full_ref[0, 2:3, rows]
        p = jnp.exp2(s * EXP_SCALE - top) * inv
        ds = (p * (dp - delta)).astype(BF16)
        p = p.astype(BF16)
        dq = (dqr_ref[0, :, rows] + mm(k_t[:, :end], ds, NN)) * SCALE
        dq_ref[rows, :] = dq.T.astype(BF16)
        dk = mm(ds, q, NN)
        dv = mm(p, do, NN)
        if chunk > 0:
            dk_acc[0:first, :] += dk[:first]
            dv_acc[0:first, :] += dv[:first]
        dk_acc[rows, :] = dk[first:]
        dv_acc[rows, :] = dv[first:]
    dk_ref[...] = (dk_acc[...] * SCALE).astype(BF16)
    dv_ref[...] = dv_acc[...].astype(BF16)


def gather_kernel(asks_ref, k_ref, v_ref, out_ref):
    for slot in range(out_ref.shape[0]):
        rows = pl.ds(pl.multiple_of(asks_ref[slot, 0] * BLOCK, BLOCK), BLOCK)
        out_ref[slot, 0:BLOCK, :] = k_ref[rows, :]
        out_ref[slot, BLOCK:, :] = v_ref[rows, :]


def add_back(here_ref, asks_ref, dk_ref, dv_ref, back_ref, acc):
    acc[0] = dk_ref[...].astype(F32)
    acc[1] = dv_ref[...].astype(F32)
    for slot in range(1, back_ref.shape[0]):

        @pl.when(slot > here_ref[0])
        def _():
            rows = pl.ds(pl.multiple_of(asks_ref[slot, 0] * BLOCK, BLOCK), BLOCK)
            acc[0, rows, :] += back_ref[slot, 0:BLOCK, :].astype(F32)
            acc[1, rows, :] += back_ref[slot, BLOCK:, :].astype(F32)


def finish_kernel(here_ref, asks_ref, dq_ref, dk_ref, dv_ref, back_ref, out_ref, acc):
    add_back(here_ref, asks_ref, dk_ref, dv_ref, back_ref, acc)
    parts, _, per_part, _ = out_ref.shape
    for which in range(2):
        out_ref[:, which] = acc[which].astype(BF16).reshape(parts, per_part, HDIM)
    out_ref[:, 2] = dq_ref[...].reshape(parts, per_part, HDIM)


def finish_pieces_kernel(here_ref, asks_ref, me_ref, dq_ref, dk_ref, dv_ref, back_ref, *refs):
    *piece_refs, acc = refs
    add_back(here_ref, asks_ref, dk_ref, dv_ref, back_ref, acc)
    for d, piece_ref in enumerate(piece_refs):
        size = piece_ref.shape[1]
        rows = pl.ds(pl.multiple_of((me_ref[0] ^ d) * size, size), size)
        for which in range(2):
            piece_ref[which] = acc[which, rows, :].astype(BF16)
        piece_ref[2] = dq_ref[rows, :]


def unpack_kernel(half, got_ref, *refs):
    *outs, sem = refs
    outs = outs[-3:]
    parts, _, _, width = got_ref.shape
    copies = []
    for part in range(parts):
        for which, out in enumerate(outs):
            cols = pl.ds((part * HALVES + half) * width, width)
            copy = pltpu.make_async_copy(got_ref.at[part, which], out.at[:, cols], sem.at[part, which])
            copy.start()
            copies.append(copy)
    for copy in copies:
        copy.wait()


def unpack_pieces_kernel(half, me_ref, *refs):
    *refs, sem = refs
    pieces, outs = refs[:-3], refs[-3:]
    width = pieces[0].shape[2]
    copies = []
    for d, piece in enumerate(pieces):
        part = me_ref[0] ^ d
        for which, out in enumerate(outs):
            cols = pl.ds(pl.multiple_of((part * HALVES + half) * width, width), width)
            copy = pltpu.make_async_copy(piece.at[which], out.at[:, cols], sem.at[d, which])
            copy.start()
            copies.append(copy)
    for copy in copies:
        copy.wait()


def params(mib=LIMIT):
    return pltpu.CompilerParams(vmem_limit_bytes=mib << 20)


def swap(array, axis):
    return lax.all_to_all(array, axis, split_axis=0, concat_axis=0, tiled=True)


def per_device(queries, key_states, value_states, out_grad, selected):
    ranges = lax.axis_size("ctx")
    members = lax.axis_size("head")
    here = lax.axis_index("ctx")
    per_dev = selected.shape[0]
    tokens, width = queries.shape
    heads = width // HDIM
    half_heads = heads // HALVES
    half_width = width // HALVES
    per_part = tokens // members
    ids = jnp.arange(ranges, dtype=jnp.int32)
    usable = selected >= 0
    owner = jnp.where(usable, selected // per_dev, -1)
    local_blk = jnp.where(usable, selected % per_dev, 0)
    from_range = owner[None] == ids[:, None, None]
    wanted = jnp.max(jnp.where(from_range, local_blk[None], 0), axis=(1, 2))
    me = lax.axis_index("head")
    wanted, here, me = lax.optimization_barrier((wanted, here, me))
    asks = swap(jnp.broadcast_to(wanted[:, None], (ranges, HDIM)), "ctx")
    here_arr = here.astype(jnp.int32).reshape(1)
    me_arr = me.astype(jnp.int32).reshape(1)

    vmem = pl.BlockSpec(memory_space=pltpu.VMEM)
    smem = pl.BlockSpec(memory_space=pltpu.SMEM)
    in_any = pl.BlockSpec(memory_space=pl.ANY)
    cols_at = lambda first: pl.BlockSpec((tokens, HDIM), lambda h: (0, first + h))
    whole = lambda a: pl.BlockSpec(a.shape, lambda h: (0,) * len(a.shape))
    per_head = lambda shape, first=0: pl.BlockSpec((1,) + shape, lambda h: (first + h, 0, 0))
    slot_cols = pl.BlockSpec((ranges, 2 * BLOCK, HDIM), lambda h: (0, 0, h))
    part_cols = lambda part: pl.BlockSpec((ranges, BLOCK, HDIM), lambda h: (0, part, h))
    pairs = tokens * tokens * half_heads
    cost = lambda dots, arrays: pl.CostEstimate(
        flops=dots * 2 * pairs * HDIM, bytes_accessed=arrays * tokens * half_width * 2, transcendentals=pairs
    )
    slots_half = jax.ShapeDtypeStruct((ranges, 2 * BLOCK, half_width), BF16)

    def gather(half, asks):
        return pl.pallas_call(
            gather_kernel,
            grid=(half_heads,),
            in_specs=[smem] + [cols_at(half * half_heads)] * 2,
            out_specs=slot_cols,
            out_shape=slots_half,
            compiler_params=params(),
        )(asks, key_states, value_states)

    sent = gather(0, asks)
    selected, here, asks, sent = lax.optimization_barrier((selected, here, asks, sent))
    owner = jnp.where(selected >= 0, selected // per_dev, -1)
    from_range = owner[None] == ids[:, None, None]
    blocks = jnp.arange(per_dev, dtype=jnp.int32)
    has_local = jnp.any(selected[None] == (here * per_dev + blocks)[:, None, None], axis=2)
    has_remote = jnp.any(from_range, axis=2) & (ids != here)[:, None]
    bias = jnp.where(jnp.concatenate([has_local, has_remote], axis=0), 0.0, MASKED).astype(F32)
    bias = jnp.repeat(bias, BLOCK, axis=1)
    bias_local, bias_remote = bias[:per_dev], bias[per_dev:]
    got = swap(sent, "ctx")
    ahead = gather(1, asks)
    stats = pl.pallas_call(
        local_stats_kernel,
        grid=(heads,),
        in_specs=[cols_at(0)] * 4 + [whole(bias_local)],
        out_specs=per_head((8, tokens)),
        out_shape=jax.ShapeDtypeStruct((heads, 8, tokens), F32),
        compiler_params=params(),
        cost_estimate=cost(4, 8),
    )(queries, out_grad, key_states, value_states, bias_local)

    def remote(half, got, ahead):
        first = half * half_heads
        return pl.pallas_call(
            remote_kernel,
            grid=(half_heads,),
            in_specs=[
                smem,
                cols_at(first),
                cols_at(first),
                part_cols(0),
                part_cols(1),
                whole(bias_remote),
                per_head((8, tokens), first),
            ]
            + [slot_cols] * len(ahead),
            out_specs=[per_head((HDIM, tokens)), slot_cols, per_head((8, tokens))],
            out_shape=[
                jax.ShapeDtypeStruct((half_heads, HDIM, tokens), F32),
                slots_half,
                jax.ShapeDtypeStruct((half_heads, 8, tokens), F32),
            ],
            scratch_shapes=[pltpu.VMEM(((ranges - 1) * BLOCK, tokens), F32)] * 2,
            compiler_params=params(),
            cost_estimate=cost(5, 8),
        )(here_arr, queries, out_grad, got, got, bias_remote, stats, *ahead)

    def local(half, full, dq_remote):
        first = half * half_heads
        return pl.pallas_call(
            local_grads_kernel,
            grid=(half_heads,),
            in_specs=[cols_at(first)] * 4
            + [whole(bias_local), per_head((8, tokens)), per_head((HDIM, tokens))],
            out_specs=[cols_at(0)] * 3,
            out_shape=[
                jax.ShapeDtypeStruct((tokens, half_width), BF16),
                jax.ShapeDtypeStruct((tokens, half_width), BF16),
                jax.ShapeDtypeStruct((tokens, half_width), BF16),
            ],
            scratch_shapes=[pltpu.VMEM((tokens, HDIM), F32)] * 2,
            compiler_params=params(),
            cost_estimate=cost(5, 10),
        )(queries, out_grad, key_states, value_states, bias_local, full, dq_remote)

    finish_cost = pl.CostEstimate(
        flops=4 * tokens * half_width, bytes_accessed=16 * tokens * half_width, transcendentals=0
    )
    finish_acc = [pltpu.VMEM((2, tokens, HDIM), F32)]
    outs_shape = [jax.ShapeDtypeStruct((per_part, members * width), BF16)] * 3
    outs_sems = [pltpu.SemaphoreType.DMA((members, 3))]

    def finish(back, grads):
        return pl.pallas_call(
            finish_kernel,
            grid=(half_heads,),
            in_specs=[smem, smem] + [cols_at(0)] * 3 + [slot_cols],
            out_specs=pl.BlockSpec((members, 3, per_part, HDIM), lambda h: (0, 0, 0, h)),
            out_shape=jax.ShapeDtypeStruct((members, 3, per_part, half_width), BF16),
            scratch_shapes=finish_acc,
            compiler_params=params(),
            cost_estimate=finish_cost,
        )(here_arr, asks, *grads, back)

    def finish_pieces(back, grads):
        return pl.pallas_call(
            finish_pieces_kernel,
            grid=(half_heads,),
            in_specs=[smem, smem, smem] + [cols_at(0)] * 3 + [slot_cols],
            out_specs=[pl.BlockSpec((3, per_part, HDIM), lambda h: (0, 0, h))] * members,
            out_shape=[jax.ShapeDtypeStruct((3, per_part, half_width), BF16)] * members,
            scratch_shapes=finish_acc,
            compiler_params=params(),
            cost_estimate=finish_cost,
        )(here_arr, asks, me_arr, *grads, back)

    def unpack_pieces(half, pieces):
        return pl.pallas_call(
            lambda *refs: unpack_pieces_kernel(half, *refs),
            in_specs=[smem] + [vmem] * members,
            out_specs=[in_any] * 3,
            out_shape=outs_shape,
            scratch_shapes=outs_sems,
            compiler_params=params(16),
        )(me_arr, *pieces)

    def unpack(half, theirs, outs):
        return pl.pallas_call(
            lambda *refs: unpack_kernel(half, *refs),
            in_specs=[vmem] + [in_any] * len(outs),
            out_specs=[in_any] * 3,
            out_shape=outs_shape,
            scratch_shapes=outs_sems,
            input_output_aliases={1 + i: i for i in range(len(outs))},
            compiler_params=params(16),
        )(theirs, *outs)

    dq0, both, full0 = remote(0, got, [ahead])
    both = swap(both, "ctx")
    own0 = local(0, full0, dq0)
    both, own0 = lax.optimization_barrier((both, own0))
    dq1, grads, full1 = remote(1, both, [])
    grads, both = lax.optimization_barrier((grads, both))
    back = swap(grads, "ctx")
    pieces = finish_pieces(both, own0)
    pieces = [pieces[0]] + [
        lax.ppermute(pieces[d], "head", [(i, i ^ d) for i in range(members)]) for d in range(1, members)
    ]
    own1 = local(1, full1, dq1)
    own1, pieces = lax.optimization_barrier((own1, pieces))
    outs = unpack_pieces(0, pieces)
    mine1 = finish(back, own1)
    key_out, value_out, query_out = unpack(1, swap(mine1, "head"), outs)
    return (query_out, key_out, value_out)


def solution(mesh):
    return jax.shard_map(
        per_device,
        mesh=mesh,
        in_specs=(
            P("ctx", "head"),
            P("ctx", "head"),
            P("ctx", "head"),
            P("ctx", "head"),
            P("ctx", None),
        ),
        out_specs=(P(("ctx", "head"), None), P(("ctx", "head"), None), P(("ctx", "head"), None)),
        check_vma=False,
    )
```

```python
import jax
import jax.numpy as jnp
from jax import lax
from jax.experimental import pallas as pl
from jax.experimental.pallas import tpu as pltpu
from jax.sharding import PartitionSpec as P

HDIM = 128
BLOCK = 64
CHUNK = 256
SCALE = 1.0 / HDIM**0.5
LOG2E = 1.4426950408889634
EXP_SCALE = SCALE * LOG2E
MASKED = -1e30
HALVES = 2
LIMIT = 63
KEY_TILE = 960
SAFE_EXPONENT = 64.0
F32 = jnp.float32
BF16 = jnp.bfloat16


def mm(a, b, dims):
    return lax.dot_general(a, b, (dims, ((), ())), preferred_element_type=F32)


NN = ((1,), (0,))
NT = ((1,), (1,))


def add_bias(scores, bias):
    keys, width = scores.shape
    blocks = keys // BLOCK
    return (scores.reshape(blocks, BLOCK, width) + bias[:, None, :]).reshape(keys, width)


def causal(scores):
    key_pos = lax.broadcasted_iota(jnp.int32, scores.shape, 0)
    query_pos = lax.broadcasted_iota(jnp.int32, scores.shape, 1)
    return jnp.where(key_pos <= query_pos, scores, MASKED)


def local_scores(k_ref, q, bias_ref, chunk):
    first = chunk * CHUNK
    last = first + CHUNK
    cols = pl.ds(first, CHUNK)
    diag = mm(k_ref[pl.ds(first, CHUNK), :], q, NT)
    diag = causal(add_bias(diag, bias_ref[pl.ds(first // BLOCK, CHUNK // BLOCK), cols]))
    if chunk == 0:
        return diag
    past = mm(k_ref[pl.ds(0, first), :], q, NT)
    past = add_bias(past, bias_ref[pl.ds(0, first // BLOCK), cols])
    return jnp.concatenate([past, diag], axis=0)


def local_stats_kernel(q_ref, do_ref, k_ref, v_ref, bias_ref, stat_ref):
    for chunk in range(q_ref.shape[0] // CHUNK):
        rows = pl.ds(chunk * CHUNK, CHUNK)
        end = (chunk + 1) * CHUNK
        s = local_scores(k_ref, q_ref[rows, :], bias_ref, chunk)
        dp = mm(v_ref[pl.ds(0, end), :], do_ref[rows, :], NT)
        top = jnp.max(s, axis=0, keepdims=True) * EXP_SCALE
        e = jnp.exp2(s * EXP_SCALE - top)
        stat_ref[0, 0:1, rows] = top
        stat_ref[0, 1:2, rows] = jnp.sum(e, axis=0, keepdims=True)
        stat_ref[0, 2:3, rows] = jnp.sum(e * dp, axis=0, keepdims=True)
        q = q_ref[rows, :].astype(F32)
        square = mm(jnp.ones((8, HDIM), BF16), (q * q).astype(BF16), NT)[0:1]
        stat_ref[0, 3:4, rows] = jnp.sqrt(square) * (1.02 * EXP_SCALE)


def remote_kernel(here_ref, q_ref, do_ref, k_ref, v_ref, bias_ref, stat_ref, *refs):
    *next_ref, dq_ref, grad_ref, full_ref, e_buf, dp_buf = refs
    slots = k_ref.shape[0] - 1
    keys = slots * BLOCK
    k = k_ref[0:slots].reshape(keys, HDIM)
    q = q_ref[...]
    do = do_ref[...]
    top_loc = stat_ref[0, 0:1, :]
    total_loc = stat_ref[0, 1:2, :]
    dot_loc = stat_ref[0, 2:3, :]

    def tiles():
        per_tile = KEY_TILE // BLOCK
        for tile in range(keys // KEY_TILE):
            at = pl.ds(tile * per_tile, per_tile)
            k_t = k_ref[at].reshape(KEY_TILE, HDIM)
            v_t = v_ref[at].reshape(KEY_TILE, HDIM)
            yield pl.ds(tile * KEY_TILE, KEY_TILE), at, mm(k_t, q, NT), mm(v_t, do, NT)

    def store(top, total, dot):
        inv = 1.0 / total
        full_ref[0, 0:1, :] = top
        full_ref[0, 1:2, :] = inv
        full_ref[0, 2:3, :] = dot * inv

    k32 = k.astype(F32)
    length = jnp.sum(k32 * k32, axis=1, keepdims=True)
    in_use = lax.broadcasted_iota(jnp.int32, length.shape, 0) < here_ref[0] * BLOCK
    longest = jnp.sqrt(jnp.max(jnp.where(in_use, length, 0.0), axis=0, keepdims=True))
    excess = jnp.max(stat_ref[0, 3:4, :] * longest - top_loc)

    @pl.when(excess < SAFE_EXPONENT)
    def _():
        total = total_loc
        dot = dot_loc
        for rows, at, s, dp in tiles():
            e = jnp.exp2(add_bias(s * EXP_SCALE, bias_ref[at, :] - top_loc))
            e_buf[rows, :] = e
            dp_buf[rows, :] = dp
            total += jnp.sum(e, axis=0, keepdims=True)
            dot += jnp.sum(e * dp, axis=0, keepdims=True)
        store(top_loc, total, dot)

    @pl.when(jnp.logical_not(excess < SAFE_EXPONENT))
    def _():
        top = top_loc
        for rows, at, s, dp in tiles():
            s = add_bias(s, bias_ref[at, :])
            e_buf[rows, :] = s
            dp_buf[rows, :] = dp
            top = jnp.maximum(top, jnp.max(s, axis=0, keepdims=True) * EXP_SCALE)
        e = jnp.exp2(e_buf[...] * EXP_SCALE - top)
        e_buf[...] = e
        keep = jnp.exp2(top_loc - top)
        total = total_loc * keep + jnp.sum(e, axis=0, keepdims=True)
        dot = dot_loc * keep + jnp.sum(e * dp_buf[...], axis=0, keepdims=True)
        store(top, total, dot)

    p = e_buf[...] * full_ref[0, 1:2, :]
    ds = (p * (dp_buf[...] - full_ref[0, 2:3, :])).astype(BF16)
    dq_ref[0] = mm(k.T, ds, NN)
    dk = mm(ds, q, NN) * SCALE
    dv = mm(p.astype(BF16), do, NN)
    grad_ref[0:slots, 0:BLOCK, :] = dk.astype(BF16).reshape(slots, BLOCK, HDIM)
    grad_ref[0:slots, BLOCK:, :] = dv.astype(BF16).reshape(slots, BLOCK, HDIM)
    grad_ref[slots] = jnp.zeros(grad_ref.shape[1:], BF16)
    for ref in next_ref:
        for slot in range(slots + 1):

            @pl.when(slot > here_ref[0])
            def _():
                grad_ref[slot] = ref[slot]


def local_grads_kernel(q_ref, do_ref, k_ref, v_ref, bias_ref, full_ref, dqr_ref, dq_ref, dk_ref, dv_ref, dk_acc, dv_acc):
    k_t = k_ref[...].T
    for chunk in range(q_ref.shape[0] // CHUNK):
        rows = pl.ds(chunk * CHUNK, CHUNK)
        first = chunk * CHUNK
        end = first + CHUNK
        q = q_ref[rows, :]
        do = do_ref[rows, :]
        s = local_scores(k_ref, q, bias_ref, chunk)
        dp = mm(v_ref[pl.ds(0, end), :], do, NT)
        top = full_ref[0, 0:1, rows]
        inv = full_ref[0, 1:2, rows]
        delta = full_ref[0, 2:3, rows]
        p = jnp.exp2(s * EXP_SCALE - top) * inv
        ds = (p * (dp - delta)).astype(BF16)
        p = p.astype(BF16)
        dq = (dqr_ref[0, :, rows] + mm(k_t[:, :end], ds, NN)) * SCALE
        dq_ref[rows, :] = dq.T.astype(BF16)
        dk = mm(ds, q, NN)
        dv = mm(p, do, NN)
        if chunk > 0:
            dk_acc[0:first, :] += dk[:first]
            dv_acc[0:first, :] += dv[:first]
        dk_acc[rows, :] = dk[first:]
        dv_acc[rows, :] = dv[first:]
    dk_ref[...] = (dk_acc[...] * SCALE).astype(BF16)
    dv_ref[...] = dv_acc[...].astype(BF16)


def gather_kernel(asks_ref, k_ref, v_ref, out_ref):
    for slot in range(out_ref.shape[0]):
        rows = pl.ds(pl.multiple_of(asks_ref[slot, 0] * BLOCK, BLOCK), BLOCK)
        out_ref[slot, 0:BLOCK, :] = k_ref[rows, :]
        out_ref[slot, BLOCK:, :] = v_ref[rows, :]


def add_back(here_ref, asks_ref, dk_ref, dv_ref, back_ref, acc):
    acc[0] = dk_ref[...].astype(F32)
    acc[1] = dv_ref[...].astype(F32)
    for slot in range(1, back_ref.shape[0]):

        @pl.when(slot > here_ref[0])
        def _():
            rows = pl.ds(pl.multiple_of(asks_ref[slot, 0] * BLOCK, BLOCK), BLOCK)
            acc[0, rows, :] += back_ref[slot, 0:BLOCK, :].astype(F32)
            acc[1, rows, :] += back_ref[slot, BLOCK:, :].astype(F32)


def finish_kernel(here_ref, asks_ref, dq_ref, dk_ref, dv_ref, back_ref, out_ref, acc):
    add_back(here_ref, asks_ref, dk_ref, dv_ref, back_ref, acc)
    parts, _, per_part, _ = out_ref.shape
    for which in range(2):
        out_ref[:, which] = acc[which].astype(BF16).reshape(parts, per_part, HDIM)
    out_ref[:, 2] = dq_ref[...].reshape(parts, per_part, HDIM)


def finish_pieces_kernel(here_ref, asks_ref, me_ref, dq_ref, dk_ref, dv_ref, back_ref, *refs):
    *piece_refs, acc = refs
    add_back(here_ref, asks_ref, dk_ref, dv_ref, back_ref, acc)
    for d, piece_ref in enumerate(piece_refs):
        size = piece_ref.shape[1]
        rows = pl.ds(pl.multiple_of((me_ref[0] ^ d) * size, size), size)
        for which in range(2):
            piece_ref[which] = acc[which, rows, :].astype(BF16)
        piece_ref[2] = dq_ref[rows, :]


def unpack_kernel(half, got_ref, *refs):
    *outs, sem = refs
    outs = outs[-3:]
    parts, _, _, width = got_ref.shape
    copies = []
    for part in range(parts):
        for which, out in enumerate(outs):
            cols = pl.ds((part * HALVES + half) * width, width)
            copy = pltpu.make_async_copy(got_ref.at[part, which], out.at[:, cols], sem.at[part, which])
            copy.start()
            copies.append(copy)
    for copy in copies:
        copy.wait()


def unpack_pieces_kernel(half, me_ref, *refs):
    *refs, sem = refs
    pieces, outs = refs[:-3], refs[-3:]
    width = pieces[0].shape[2]
    copies = []
    for d, piece in enumerate(pieces):
        part = me_ref[0] ^ d
        for which, out in enumerate(outs):
            cols = pl.ds(pl.multiple_of((part * HALVES + half) * width, width), width)
            copy = pltpu.make_async_copy(piece.at[which], out.at[:, cols], sem.at[d, which])
            copy.start()
            copies.append(copy)
    for copy in copies:
        copy.wait()


def params(mib=LIMIT):
    return pltpu.CompilerParams(vmem_limit_bytes=mib << 20)


def swap(array, axis):
    return lax.all_to_all(array, axis, split_axis=0, concat_axis=0, tiled=True)


def per_device(queries, key_states, value_states, out_grad, selected):
    ranges = lax.axis_size("ctx")
    members = lax.axis_size("head")
    here = lax.axis_index("ctx")
    per_dev = selected.shape[0]
    tokens, width = queries.shape
    heads = width // HDIM
    half_heads = heads // HALVES
    half_width = width // HALVES
    per_part = tokens // members
    ids = jnp.arange(ranges, dtype=jnp.int32)
    usable = selected >= 0
    owner = jnp.where(usable, selected // per_dev, -1)
    local_blk = jnp.where(usable, selected % per_dev, 0)
    from_range = owner[None] == ids[:, None, None]
    wanted = jnp.max(jnp.where(from_range, local_blk[None], 0), axis=(1, 2))
    me = lax.axis_index("head")
    wanted, here, me = lax.optimization_barrier((wanted, here, me))
    asks = swap(jnp.broadcast_to(wanted[:, None], (ranges, HDIM)), "ctx")
    here_arr = here.astype(jnp.int32).reshape(1)
    me_arr = me.astype(jnp.int32).reshape(1)

    vmem = pl.BlockSpec(memory_space=pltpu.VMEM)
    smem = pl.BlockSpec(memory_space=pltpu.SMEM)
    in_any = pl.BlockSpec(memory_space=pl.ANY)
    cols_at = lambda first: pl.BlockSpec((tokens, HDIM), lambda h: (0, first + h))
    whole = lambda a: pl.BlockSpec(a.shape, lambda h: (0,) * len(a.shape))
    per_head = lambda shape, first=0: pl.BlockSpec((1,) + shape, lambda h: (first + h, 0, 0))
    slot_cols = pl.BlockSpec((ranges, 2 * BLOCK, HDIM), lambda h: (0, 0, h))
    part_cols = lambda part: pl.BlockSpec((ranges, BLOCK, HDIM), lambda h: (0, part, h))
    pairs = tokens * tokens * half_heads
    cost = lambda dots, arrays: pl.CostEstimate(
        flops=dots * 2 * pairs * HDIM, bytes_accessed=arrays * tokens * half_width * 2, transcendentals=pairs
    )
    slots_half = jax.ShapeDtypeStruct((ranges, 2 * BLOCK, half_width), BF16)

    def gather(half, asks):
        return pl.pallas_call(
            gather_kernel,
            grid=(half_heads,),
            in_specs=[smem] + [cols_at(half * half_heads)] * 2,
            out_specs=slot_cols,
            out_shape=slots_half,
            compiler_params=params(),
        )(asks, key_states, value_states)

    sent = gather(0, asks)
    asks, sent = lax.optimization_barrier((asks, sent))
    ahead = gather(1, asks)
    selected, here, ahead = lax.optimization_barrier((selected, here, ahead))
    owner = jnp.where(selected >= 0, selected // per_dev, -1)
    from_range = owner[None] == ids[:, None, None]
    blocks = jnp.arange(per_dev, dtype=jnp.int32)
    has_local = jnp.any(selected[None] == (here * per_dev + blocks)[:, None, None], axis=2)
    has_remote = jnp.any(from_range, axis=2) & (ids != here)[:, None]
    bias = jnp.where(jnp.concatenate([has_local, has_remote], axis=0), 0.0, MASKED).astype(F32)
    bias = jnp.repeat(bias, BLOCK, axis=1)
    bias_local, bias_remote = bias[:per_dev], bias[per_dev:]
    got = swap(sent, "ctx")
    stats = pl.pallas_call(
        local_stats_kernel,
        grid=(heads,),
        in_specs=[cols_at(0)] * 4 + [whole(bias_local)],
        out_specs=per_head((8, tokens)),
        out_shape=jax.ShapeDtypeStruct((heads, 8, tokens), F32),
        compiler_params=params(),
        cost_estimate=cost(4, 8),
    )(queries, out_grad, key_states, value_states, bias_local)

    def remote(half, got, ahead):
        first = half * half_heads
        return pl.pallas_call(
            remote_kernel,
            grid=(half_heads,),
            in_specs=[
                smem,
                cols_at(first),
                cols_at(first),
                part_cols(0),
                part_cols(1),
                whole(bias_remote),
                per_head((8, tokens), first),
            ]
            + [slot_cols] * len(ahead),
            out_specs=[per_head((HDIM, tokens)), slot_cols, per_head((8, tokens))],
            out_shape=[
                jax.ShapeDtypeStruct((half_heads, HDIM, tokens), F32),
                slots_half,
                jax.ShapeDtypeStruct((half_heads, 8, tokens), F32),
            ],
            scratch_shapes=[pltpu.VMEM(((ranges - 1) * BLOCK, tokens), F32)] * 2,
            compiler_params=params(),
            cost_estimate=cost(5, 8),
        )(here_arr, queries, out_grad, got, got, bias_remote, stats, *ahead)

    def local(half, full, dq_remote):
        first = half * half_heads
        return pl.pallas_call(
            local_grads_kernel,
            grid=(half_heads,),
            in_specs=[cols_at(first)] * 4
            + [whole(bias_local), per_head((8, tokens)), per_head((HDIM, tokens))],
            out_specs=[cols_at(0)] * 3,
            out_shape=[
                jax.ShapeDtypeStruct((tokens, half_width), BF16),
                jax.ShapeDtypeStruct((tokens, half_width), BF16),
                jax.ShapeDtypeStruct((tokens, half_width), BF16),
            ],
            scratch_shapes=[pltpu.VMEM((tokens, HDIM), F32)] * 2,
            compiler_params=params(),
            cost_estimate=cost(5, 10),
        )(queries, out_grad, key_states, value_states, bias_local, full, dq_remote)

    finish_cost = pl.CostEstimate(
        flops=4 * tokens * half_width, bytes_accessed=16 * tokens * half_width, transcendentals=0
    )
    finish_acc = [pltpu.VMEM((2, tokens, HDIM), F32)]
    outs_shape = [jax.ShapeDtypeStruct((per_part, members * width), BF16)] * 3
    outs_sems = [pltpu.SemaphoreType.DMA((members, 3))]

    def finish(back, grads):
        return pl.pallas_call(
            finish_kernel,
            grid=(half_heads,),
            in_specs=[smem, smem] + [cols_at(0)] * 3 + [slot_cols],
            out_specs=pl.BlockSpec((members, 3, per_part, HDIM), lambda h: (0, 0, 0, h)),
            out_shape=jax.ShapeDtypeStruct((members, 3, per_part, half_width), BF16),
            scratch_shapes=finish_acc,
            compiler_params=params(),
            cost_estimate=finish_cost,
        )(here_arr, asks, *grads, back)

    def finish_pieces(back, grads):
        return pl.pallas_call(
            finish_pieces_kernel,
            grid=(half_heads,),
            in_specs=[smem, smem, smem] + [cols_at(0)] * 3 + [slot_cols],
            out_specs=[pl.BlockSpec((3, per_part, HDIM), lambda h: (0, 0, h))] * members,
            out_shape=[jax.ShapeDtypeStruct((3, per_part, half_width), BF16)] * members,
            scratch_shapes=finish_acc,
            compiler_params=params(),
            cost_estimate=finish_cost,
        )(here_arr, asks, me_arr, *grads, back)

    def unpack_pieces(half, pieces):
        return pl.pallas_call(
            lambda *refs: unpack_pieces_kernel(half, *refs),
            in_specs=[smem] + [vmem] * members,
            out_specs=[in_any] * 3,
            out_shape=outs_shape,
            scratch_shapes=outs_sems,
            compiler_params=params(16),
        )(me_arr, *pieces)

    def unpack(half, theirs, outs):
        return pl.pallas_call(
            lambda *refs: unpack_kernel(half, *refs),
            in_specs=[vmem] + [in_any] * len(outs),
            out_specs=[in_any] * 3,
            out_shape=outs_shape,
            scratch_shapes=outs_sems,
            input_output_aliases={1 + i: i for i in range(len(outs))},
            compiler_params=params(16),
        )(theirs, *outs)

    dq0, both, full0 = remote(0, got, [ahead])
    both = swap(both, "ctx")
    own0 = local(0, full0, dq0)
    both, own0 = lax.optimization_barrier((both, own0))
    dq1, grads, full1 = remote(1, both, [])
    grads, both = lax.optimization_barrier((grads, both))
    back = swap(grads, "ctx")
    pieces = finish_pieces(both, own0)
    pieces = [pieces[0]] + [
        lax.ppermute(pieces[d], "head", [(i, i ^ d) for i in range(members)]) for d in range(1, members)
    ]
    own1 = local(1, full1, dq1)
    own1, pieces = lax.optimization_barrier((own1, pieces))
    outs = unpack_pieces(0, pieces)
    mine1 = finish(back, own1)
    key_out, value_out, query_out = unpack(1, swap(mine1, "head"), outs)
    return (query_out, key_out, value_out)


def solution(mesh):
    return jax.shard_map(
        per_device,
        mesh=mesh,
        in_specs=(
            P("ctx", "head"),
            P("ctx", "head"),
            P("ctx", "head"),
            P("ctx", "head"),
            P("ctx", None),
        ),
        out_specs=(P(("ctx", "head"), None), P(("ctx", "head"), None), P(("ctx", "head"), None)),
        check_vma=False,
    )
```

```python
import jax
import jax.numpy as jnp
from jax import lax
from jax.experimental import pallas as pl
from jax.experimental.pallas import tpu as pltpu
from jax.sharding import PartitionSpec as P

HDIM = 128
BLOCK = 64
CHUNK = 256
SCALE = 1.0 / HDIM**0.5
LOG2E = 1.4426950408889634
EXP_SCALE = SCALE * LOG2E
MASKED = -1e30
HALVES = 2
LIMIT = 63
KEY_TILE = 960
SAFE_EXPONENT = 64.0
F32 = jnp.float32
BF16 = jnp.bfloat16


def mm(a, b, dims):
    return lax.dot_general(a, b, (dims, ((), ())), preferred_element_type=F32)


NN = ((1,), (0,))
NT = ((1,), (1,))


def add_bias(scores, bias):
    keys, width = scores.shape
    blocks = keys // BLOCK
    return (scores.reshape(blocks, BLOCK, width) + bias[:, None, :]).reshape(keys, width)


def causal(scores):
    key_pos = lax.broadcasted_iota(jnp.int32, scores.shape, 0)
    query_pos = lax.broadcasted_iota(jnp.int32, scores.shape, 1)
    return jnp.where(key_pos <= query_pos, scores, MASKED)


def local_scores(k_ref, q, bias_ref, chunk):
    first = chunk * CHUNK
    last = first + CHUNK
    cols = pl.ds(first, CHUNK)
    diag = mm(k_ref[pl.ds(first, CHUNK), :], q, NT)
    diag = causal(add_bias(diag, bias_ref[pl.ds(first // BLOCK, CHUNK // BLOCK), cols]))
    if chunk == 0:
        return diag
    past = mm(k_ref[pl.ds(0, first), :], q, NT)
    past = add_bias(past, bias_ref[pl.ds(0, first // BLOCK), cols])
    return jnp.concatenate([past, diag], axis=0)


def local_stats_kernel(q_ref, do_ref, k_ref, v_ref, bias_ref, stat_ref):
    for chunk in range(q_ref.shape[0] // CHUNK):
        rows = pl.ds(chunk * CHUNK, CHUNK)
        end = (chunk + 1) * CHUNK
        s = local_scores(k_ref, q_ref[rows, :], bias_ref, chunk)
        dp = mm(v_ref[pl.ds(0, end), :], do_ref[rows, :], NT)
        top = jnp.max(s, axis=0, keepdims=True) * EXP_SCALE
        e = jnp.exp2(s * EXP_SCALE - top)
        stat_ref[0, 0:1, rows] = top
        stat_ref[0, 1:2, rows] = jnp.sum(e, axis=0, keepdims=True)
        stat_ref[0, 2:3, rows] = jnp.sum(e * dp, axis=0, keepdims=True)
        q = q_ref[rows, :].astype(F32)
        square = mm(jnp.ones((8, HDIM), BF16), (q * q).astype(BF16), NT)[0:1]
        stat_ref[0, 3:4, rows] = jnp.sqrt(square) * (1.02 * EXP_SCALE)


def remote_kernel(here_ref, q_ref, do_ref, k_ref, v_ref, bias_ref, stat_ref, *refs):
    *next_ref, dq_ref, grad_ref, full_ref, e_buf, dp_buf = refs
    slots = k_ref.shape[0] - 1
    keys = slots * BLOCK
    k = k_ref[0:slots].reshape(keys, HDIM)
    q = q_ref[...]
    do = do_ref[...]
    top_loc = stat_ref[0, 0:1, :]
    total_loc = stat_ref[0, 1:2, :]
    dot_loc = stat_ref[0, 2:3, :]

    def tiles():
        per_tile = KEY_TILE // BLOCK
        for tile in range(keys // KEY_TILE):
            at = pl.ds(tile * per_tile, per_tile)
            k_t = k_ref[at].reshape(KEY_TILE, HDIM)
            v_t = v_ref[at].reshape(KEY_TILE, HDIM)
            yield pl.ds(tile * KEY_TILE, KEY_TILE), at, mm(k_t, q, NT), mm(v_t, do, NT)

    def store(top, total, dot):
        inv = 1.0 / total
        full_ref[0, 0:1, :] = top
        full_ref[0, 1:2, :] = inv
        full_ref[0, 2:3, :] = dot * inv

    k32 = k.astype(F32)
    length = jnp.sum(k32 * k32, axis=1, keepdims=True)
    in_use = lax.broadcasted_iota(jnp.int32, length.shape, 0) < here_ref[0] * BLOCK
    longest = jnp.sqrt(jnp.max(jnp.where(in_use, length, 0.0), axis=0, keepdims=True))
    excess = jnp.max(stat_ref[0, 3:4, :] * longest - top_loc)

    @pl.when(excess < SAFE_EXPONENT)
    def _():
        total = total_loc
        dot = dot_loc
        for rows, at, s, dp in tiles():
            e = jnp.exp2(add_bias(s * EXP_SCALE, bias_ref[at, :] - top_loc))
            e_buf[rows, :] = e
            dp_buf[rows, :] = dp
            total += jnp.sum(e, axis=0, keepdims=True)
            dot += jnp.sum(e * dp, axis=0, keepdims=True)
        store(top_loc, total, dot)

    @pl.when(jnp.logical_not(excess < SAFE_EXPONENT))
    def _():
        top = top_loc
        for rows, at, s, dp in tiles():
            s = add_bias(s, bias_ref[at, :])
            e_buf[rows, :] = s
            dp_buf[rows, :] = dp
            top = jnp.maximum(top, jnp.max(s, axis=0, keepdims=True) * EXP_SCALE)
        e = jnp.exp2(e_buf[...] * EXP_SCALE - top)
        e_buf[...] = e
        keep = jnp.exp2(top_loc - top)
        total = total_loc * keep + jnp.sum(e, axis=0, keepdims=True)
        dot = dot_loc * keep + jnp.sum(e * dp_buf[...], axis=0, keepdims=True)
        store(top, total, dot)

    p = e_buf[...] * full_ref[0, 1:2, :]
    ds = (p * (dp_buf[...] - full_ref[0, 2:3, :])).astype(BF16)
    dq_ref[0] = mm(k.T, ds, NN)
    dk = mm(ds, q, NN) * SCALE
    dv = mm(p.astype(BF16), do, NN)
    grad_ref[0:slots, 0:BLOCK, :] = dk.astype(BF16).reshape(slots, BLOCK, HDIM)
    grad_ref[0:slots, BLOCK:, :] = dv.astype(BF16).reshape(slots, BLOCK, HDIM)
    grad_ref[slots] = jnp.zeros(grad_ref.shape[1:], BF16)
    for ref in next_ref:
        for slot in range(slots + 1):

            @pl.when(slot > here_ref[0])
            def _():
                grad_ref[slot] = ref[slot]


def local_grads_kernel(q_ref, do_ref, k_ref, v_ref, bias_ref, full_ref, dqr_ref, dq_ref, dk_ref, dv_ref, dk_acc, dv_acc):
    k_t = k_ref[...].T
    for chunk in range(q_ref.shape[0] // CHUNK):
        rows = pl.ds(chunk * CHUNK, CHUNK)
        first = chunk * CHUNK
        end = first + CHUNK
        q = q_ref[rows, :]
        do = do_ref[rows, :]
        s = local_scores(k_ref, q, bias_ref, chunk)
        dp = mm(v_ref[pl.ds(0, end), :], do, NT)
        top = full_ref[0, 0:1, rows]
        inv = full_ref[0, 1:2, rows]
        delta = full_ref[0, 2:3, rows]
        p = jnp.exp2(s * EXP_SCALE - top) * inv
        ds = (p * (dp - delta)).astype(BF16)
        p = p.astype(BF16)
        dq = (dqr_ref[0, :, rows] + mm(k_t[:, :end], ds, NN)) * SCALE
        dq_ref[rows, :] = dq.T.astype(BF16)
        dk = mm(ds, q, NN)
        dv = mm(p, do, NN)
        if chunk > 0:
            dk_acc[0:first, :] += dk[:first]
            dv_acc[0:first, :] += dv[:first]
        dk_acc[rows, :] = dk[first:]
        dv_acc[rows, :] = dv[first:]
    dk_ref[...] = (dk_acc[...] * SCALE).astype(BF16)
    dv_ref[...] = dv_acc[...].astype(BF16)


def gather_kernel(asks_ref, k_ref, v_ref, out_ref):
    for slot in range(out_ref.shape[0]):
        rows = pl.ds(pl.multiple_of(asks_ref[slot, 0] * BLOCK, BLOCK), BLOCK)
        out_ref[slot, 0:BLOCK, :] = k_ref[rows, :]
        out_ref[slot, BLOCK:, :] = v_ref[rows, :]


def add_back(here_ref, asks_ref, dk_ref, dv_ref, back_ref, acc):
    acc[0] = dk_ref[...].astype(F32)
    acc[1] = dv_ref[...].astype(F32)
    for slot in range(1, back_ref.shape[0]):

        @pl.when(slot > here_ref[0])
        def _():
            rows = pl.ds(pl.multiple_of(asks_ref[slot, 0] * BLOCK, BLOCK), BLOCK)
            acc[0, rows, :] += back_ref[slot, 0:BLOCK, :].astype(F32)
            acc[1, rows, :] += back_ref[slot, BLOCK:, :].astype(F32)


def finish_kernel(here_ref, asks_ref, dq_ref, dk_ref, dv_ref, back_ref, out_ref, acc):
    add_back(here_ref, asks_ref, dk_ref, dv_ref, back_ref, acc)
    parts, _, per_part, _ = out_ref.shape
    for which in range(2):
        out_ref[:, which] = acc[which].astype(BF16).reshape(parts, per_part, HDIM)
    out_ref[:, 2] = dq_ref[...].reshape(parts, per_part, HDIM)


def partners(members):
    return sorted(range(members), key=lambda d: (d >= members // 2, d % 4 == 2, d))


def finish_pieces_kernel(here_ref, asks_ref, me_ref, dq_ref, dk_ref, dv_ref, back_ref, *refs):
    *piece_refs, acc = refs
    add_back(here_ref, asks_ref, dk_ref, dv_ref, back_ref, acc)
    for d, piece_ref in zip(partners(len(piece_refs)), piece_refs):
        size = piece_ref.shape[1]
        rows = pl.ds(pl.multiple_of((me_ref[0] ^ d) * size, size), size)
        for which in range(2):
            piece_ref[which] = acc[which, rows, :].astype(BF16)
        piece_ref[2] = dq_ref[rows, :]


def unpack_kernel(half, got_ref, *refs):
    *outs, sem = refs
    outs = outs[-3:]
    parts, _, _, width = got_ref.shape
    copies = []
    for part in range(parts):
        for which, out in enumerate(outs):
            cols = pl.ds((part * HALVES + half) * width, width)
            copy = pltpu.make_async_copy(got_ref.at[part, which], out.at[:, cols], sem.at[part, which])
            copy.start()
            copies.append(copy)
    for copy in copies:
        copy.wait()


def unpack_pieces_kernel(half, me_ref, *refs):
    *refs, sem = refs
    pieces, outs = refs[:-3], refs[-3:]
    width = pieces[0].shape[2]
    copies = []
    for d, piece in zip(partners(len(pieces)), pieces):
        part = me_ref[0] ^ d
        for which, out in enumerate(outs):
            cols = pl.ds(pl.multiple_of((part * HALVES + half) * width, width), width)
            copy = pltpu.make_async_copy(piece.at[which], out.at[:, cols], sem.at[d, which])
            copy.start()
            copies.append(copy)
    for copy in copies:
        copy.wait()


def params(mib=LIMIT):
    return pltpu.CompilerParams(vmem_limit_bytes=mib << 20)


def swap(array, axis):
    return lax.all_to_all(array, axis, split_axis=0, concat_axis=0, tiled=True)


def per_device(queries, key_states, value_states, out_grad, selected):
    ranges = lax.axis_size("ctx")
    members = lax.axis_size("head")
    here = lax.axis_index("ctx")
    per_dev = selected.shape[0]
    tokens, width = queries.shape
    heads = width // HDIM
    half_heads = heads // HALVES
    half_width = width // HALVES
    per_part = tokens // members
    ids = jnp.arange(ranges, dtype=jnp.int32)
    usable = selected >= 0
    owner = jnp.where(usable, selected // per_dev, -1)
    local_blk = jnp.where(usable, selected % per_dev, 0)
    from_range = owner[None] == ids[:, None, None]
    wanted = jnp.max(jnp.where(from_range, local_blk[None], 0), axis=(1, 2))
    me = lax.axis_index("head")
    wanted, here, me = lax.optimization_barrier((wanted, here, me))
    asks = swap(jnp.broadcast_to(wanted[:, None], (ranges, HDIM)), "ctx")
    here_arr = here.astype(jnp.int32).reshape(1)
    me_arr = me.astype(jnp.int32).reshape(1)

    vmem = pl.BlockSpec(memory_space=pltpu.VMEM)
    smem = pl.BlockSpec(memory_space=pltpu.SMEM)
    in_any = pl.BlockSpec(memory_space=pl.ANY)
    cols_at = lambda first: pl.BlockSpec((tokens, HDIM), lambda h: (0, first + h))
    whole = lambda a: pl.BlockSpec(a.shape, lambda h: (0,) * len(a.shape))
    per_head = lambda shape, first=0: pl.BlockSpec((1,) + shape, lambda h: (first + h, 0, 0))
    slot_cols = pl.BlockSpec((ranges, 2 * BLOCK, HDIM), lambda h: (0, 0, h))
    part_cols = lambda part: pl.BlockSpec((ranges, BLOCK, HDIM), lambda h: (0, part, h))
    pairs = tokens * tokens * half_heads
    cost = lambda dots, arrays: pl.CostEstimate(
        flops=dots * 2 * pairs * HDIM, bytes_accessed=arrays * tokens * half_width * 2, transcendentals=pairs
    )
    slots_half = jax.ShapeDtypeStruct((ranges, 2 * BLOCK, half_width), BF16)

    def gather(half, asks):
        return pl.pallas_call(
            gather_kernel,
            grid=(half_heads,),
            in_specs=[smem] + [cols_at(half * half_heads)] * 2,
            out_specs=slot_cols,
            out_shape=slots_half,
            compiler_params=params(),
        )(asks, key_states, value_states)

    sent = gather(0, asks)
    asks, sent = lax.optimization_barrier((asks, sent))
    ahead = gather(1, asks)
    selected, here, ahead = lax.optimization_barrier((selected, here, ahead))
    owner = jnp.where(selected >= 0, selected // per_dev, -1)
    from_range = owner[None] == ids[:, None, None]
    blocks = jnp.arange(per_dev, dtype=jnp.int32)
    has_local = jnp.any(selected[None] == (here * per_dev + blocks)[:, None, None], axis=2)
    has_remote = jnp.any(from_range, axis=2) & (ids != here)[:, None]
    bias = jnp.where(jnp.concatenate([has_local, has_remote], axis=0), 0.0, MASKED).astype(F32)
    bias = jnp.repeat(bias, BLOCK, axis=1)
    bias_local, bias_remote = bias[:per_dev], bias[per_dev:]
    got = swap(sent, "ctx")
    stats = pl.pallas_call(
        local_stats_kernel,
        grid=(heads,),
        in_specs=[cols_at(0)] * 4 + [whole(bias_local)],
        out_specs=per_head((8, tokens)),
        out_shape=jax.ShapeDtypeStruct((heads, 8, tokens), F32),
        compiler_params=params(),
        cost_estimate=cost(4, 8),
    )(queries, out_grad, key_states, value_states, bias_local)

    def remote(half, got, ahead):
        first = half * half_heads
        return pl.pallas_call(
            remote_kernel,
            grid=(half_heads,),
            in_specs=[
                smem,
                cols_at(first),
                cols_at(first),
                part_cols(0),
                part_cols(1),
                whole(bias_remote),
                per_head((8, tokens), first),
            ]
            + [slot_cols] * len(ahead),
            out_specs=[per_head((HDIM, tokens)), slot_cols, per_head((8, tokens))],
            out_shape=[
                jax.ShapeDtypeStruct((half_heads, HDIM, tokens), F32),
                slots_half,
                jax.ShapeDtypeStruct((half_heads, 8, tokens), F32),
            ],
            scratch_shapes=[pltpu.VMEM(((ranges - 1) * BLOCK, tokens), F32)] * 2,
            compiler_params=params(),
            cost_estimate=cost(5, 8),
        )(here_arr, queries, out_grad, got, got, bias_remote, stats, *ahead)

    def local(half, full, dq_remote):
        first = half * half_heads
        return pl.pallas_call(
            local_grads_kernel,
            grid=(half_heads,),
            in_specs=[cols_at(first)] * 4
            + [whole(bias_local), per_head((8, tokens)), per_head((HDIM, tokens))],
            out_specs=[cols_at(0)] * 3,
            out_shape=[
                jax.ShapeDtypeStruct((tokens, half_width), BF16),
                jax.ShapeDtypeStruct((tokens, half_width), BF16),
                jax.ShapeDtypeStruct((tokens, half_width), BF16),
            ],
            scratch_shapes=[pltpu.VMEM((tokens, HDIM), F32)] * 2,
            compiler_params=params(),
            cost_estimate=cost(5, 10),
        )(queries, out_grad, key_states, value_states, bias_local, full, dq_remote)

    finish_cost = pl.CostEstimate(
        flops=4 * tokens * half_width, bytes_accessed=16 * tokens * half_width, transcendentals=0
    )
    finish_acc = [pltpu.VMEM((2, tokens, HDIM), F32)]
    outs_shape = [jax.ShapeDtypeStruct((per_part, members * width), BF16)] * 3
    outs_sems = [pltpu.SemaphoreType.DMA((members, 3))]

    def finish(back, grads):
        return pl.pallas_call(
            finish_kernel,
            grid=(half_heads,),
            in_specs=[smem, smem] + [cols_at(0)] * 3 + [slot_cols],
            out_specs=pl.BlockSpec((members, 3, per_part, HDIM), lambda h: (0, 0, 0, h)),
            out_shape=jax.ShapeDtypeStruct((members, 3, per_part, half_width), BF16),
            scratch_shapes=finish_acc,
            compiler_params=params(),
            cost_estimate=finish_cost,
        )(here_arr, asks, *grads, back)

    def finish_pieces(back, grads):
        return pl.pallas_call(
            finish_pieces_kernel,
            grid=(half_heads,),
            in_specs=[smem, smem, smem] + [cols_at(0)] * 3 + [slot_cols],
            out_specs=[pl.BlockSpec((3, per_part, HDIM), lambda h: (0, 0, h))] * members,
            out_shape=[jax.ShapeDtypeStruct((3, per_part, half_width), BF16)] * members,
            scratch_shapes=finish_acc,
            compiler_params=params(),
            cost_estimate=finish_cost,
        )(here_arr, asks, me_arr, *grads, back)

    def unpack_pieces(half, pieces):
        return pl.pallas_call(
            lambda *refs: unpack_pieces_kernel(half, *refs),
            in_specs=[smem] + [vmem] * members,
            out_specs=[in_any] * 3,
            out_shape=outs_shape,
            scratch_shapes=outs_sems,
            compiler_params=params(16),
        )(me_arr, *pieces)

    def unpack(half, theirs, outs):
        return pl.pallas_call(
            lambda *refs: unpack_kernel(half, *refs),
            in_specs=[vmem] + [in_any] * len(outs),
            out_specs=[in_any] * 3,
            out_shape=outs_shape,
            scratch_shapes=outs_sems,
            input_output_aliases={1 + i: i for i in range(len(outs))},
            compiler_params=params(16),
        )(theirs, *outs)

    dq0, both, full0 = remote(0, got, [ahead])
    both = swap(both, "ctx")
    own0 = local(0, full0, dq0)
    both, own0 = lax.optimization_barrier((both, own0))
    dq1, grads, full1 = remote(1, both, [])
    grads, both = lax.optimization_barrier((grads, both))
    back = swap(grads, "ctx")
    pieces = finish_pieces(both, own0)
    pieces = [
        lax.ppermute(piece, "head", [(i, i ^ d) for i in range(members)]) if d else piece
        for d, piece in zip(partners(members), pieces)
    ]
    own1 = local(1, full1, dq1)
    own1, pieces = lax.optimization_barrier((own1, pieces))
    outs = unpack_pieces(0, pieces)
    mine1 = finish(back, own1)
    key_out, value_out, query_out = unpack(1, swap(mine1, "head"), outs)
    return (query_out, key_out, value_out)


def solution(mesh):
    return jax.shard_map(
        per_device,
        mesh=mesh,
        in_specs=(
            P("ctx", "head"),
            P("ctx", "head"),
            P("ctx", "head"),
            P("ctx", "head"),
            P("ctx", None),
        ),
        out_specs=(P(("ctx", "head"), None), P(("ctx", "head"), None), P(("ctx", "head"), None)),
        check_vma=False,
    )
```
